32 devices in a mesh: groups: 2 (over y), vel: 4 (over z), cell: 2 (over x), sub: 2 (over core).
Axes of the slice: x: 2, y: 2, z: 4, core: 2. Of those that a mesh axis runs over, the one named last changes fastest.
Arguments:
- density: bfloat16 [768, 110592], P(('groups', 'cell', 'sub'), 'vel'), parts along dimension 0, may hold values from 0.5 to 1.5
- coder: bfloat16 [110592, 512], P('vel'), may hold values from -0.01953125 to 0.01953125
- w_latent: bfloat16 [512, 512], replicated, may hold values from -0.25 to 0.25
- b_latent: float32 [512], replicated, may hold values from -3 to 3
- restitution: float32 [768], P(('groups', 'cell', 'sub')), parts along dimension 0, may hold values from 0.3 to 0.95
- inflow: float32 [221184], P(('groups', 'vel')), parts along dimension 0, may hold values from 0.5 to 1.5
- flags: int32 [8], P('groups'), parts along dimension 0, may hold values from 0 to 1, as said below
- blocks: int32 [192], P(('groups', 'vel')), parts along dimension 0, may hold values from 0 to 95, each once
Outputs:
- density_out: bfloat16 [768, 110592], P(('groups', 'cell', 'sub'), 'vel'), parts along dimension 0
The draws below stay inside these ranges and needn't reach their ends.
There are 2 independent parts, one for each index of `groups`. The reference program is written for one: setup_inputs(seed, part) draws one part's arguments, and reference() takes and returns one part's arrays. A program takes and returns all parts, laid end to end along the dimension named above; an argument that names none is the same for every part. Nothing has to cross between parts.
Inputs may be any that keep to these rules, and one draw needn't show every extreme that they name: flags[b] = 1 joins block b of 96 cells to block b - 1 (block 0 to the last block); 0 makes that boundary an inflow boundary. Every draw holds both values. A permutation of the velocity blocks.
All inputs are finite; a program needn't handle non-finite values.
Results may differ from the reference program's by a relative error of at most 0.007.
Values may be sent and summed in bfloat16 or wider, within the bound.
No kernel may reach another device: no remote copies, remote signals or barrier semaphores. Data moves between devices by JAX's collectives and lax.ppermute only.
A program may use at most 128 MiB of HBM per device.

```python
import math
import jax
import jax.numpy as jnp
import numpy as np
from jax import lax

VGRID = 48
LATENT = 512
VBLOCKS = 96
STEPS = 2
C_DEV = 96
VELS = 110592
BLOCKS = 4
CELLS = 384


def draw_flags(key, part):
    first, second, third = jax.random.split(jax.random.fold_in(key, 7), 3)
    base = (jax.random.randint(first, (BLOCKS,), 0, 4) > 0).astype(jnp.int32)
    closed = jax.random.randint(second, (), 0, BLOCKS)
    opened = (closed + 1 + jax.random.randint(third, (), 0, BLOCKS - 1)) % BLOCKS
    marks = jnp.arange(BLOCKS, dtype=jnp.int32)
    base = jnp.where(marks == closed, 0, base)
    base = jnp.where(marks == opened, 1, base)
    return base.astype(jnp.int32)


def level_of(key, extent, cuts, low, high):
    level = 1.0
    for position, shards_of in cuts:
        draws = jax.random.uniform(jax.random.fold_in(jax.random.fold_in(key, 6), position), (shards_of,), jnp.float32, low / len(cuts), high / len(cuts))
        level = level * jnp.repeat(jnp.exp(draws), extent[position] // shards_of).reshape((-1,) + (1,) * (len(extent) - 1 - position))
    return level


def centred(own_key, extent, scale, reach, cuts=(), held_as=jnp.bfloat16):
    array = scale * jax.random.normal(own_key, extent, jnp.float32)
    if cuts:
        array = array * level_of(own_key, extent, cuts, -0.22, 0.18)
    return jnp.clip(array, -reach, reach).astype(held_as)


def setup_inputs(seed: int = 0, part: int = 0) -> dict:
    arg_keys = jax.random.split(jax.random.key(seed), 9)
    own_keys = jax.random.split(jax.random.fold_in(arg_keys[8], part), 9)
    density = jnp.clip(0.5 + 1.0 * jax.random.uniform(own_keys[0], (CELLS, VELS), jnp.float32) ** level_of(own_keys[0], (CELLS, VELS), ((0, 4), (1, 4)), -0.2, 0.2), 0.5, 1.5).astype(jnp.bfloat16)
    coder = centred(arg_keys[1], (VELS, LATENT), VELS ** -0.5, 0.01953125, ((0, 4),))
    w_latent = centred(arg_keys[2], (LATENT, LATENT), LATENT ** -0.5, 0.25)
    b_latent = centred(arg_keys[3], (LATENT,), 0.5, 3.0, (), jnp.float32)
    restitution = jnp.clip(0.3 + 0.65 * jax.random.uniform(own_keys[4], (CELLS,), jnp.float32) ** level_of(own_keys[4], (CELLS,), ((0, 4),), -0.2, 0.2), 0.3, 0.95)
    inflow = jnp.clip(0.5 + 1.0 * jax.random.uniform(own_keys[5], (VELS,), jnp.float32) ** level_of(own_keys[5], (VELS,), ((0, 4),), -0.2, 0.2), 0.5, 1.5)
    flags = draw_flags(jax.random.fold_in(jax.random.fold_in(arg_keys[8], part), 71), part)
    blocks = jax.random.permutation(own_keys[7], VBLOCKS).astype(jnp.int32)
    return {"density": density, "coder": coder, "w_latent": w_latent, "b_latent": b_latent, "restitution": restitution, "inflow": inflow, "flags": flags, "blocks": blocks}


SINK_RATE = 0.5
COURANT = 0.9

def grid_moments():
    centres = (2.0 * np.arange(VGRID) + 1.0 - VGRID) / VGRID
    second = float(np.sum(centres ** 2))
    fourth = float(np.sum(centres ** 4))
    number = float(VGRID)
    total = number ** 3
    cross = 3.0 * number * number * second
    quartic = 3.0 * number * number * fourth + 6.0 * number * second * second
    square = number * number * second
    return (total, cross, quartic, square)

def component(number):
    return (2 * number + 1 - VGRID).astype(jnp.float32) / VGRID

def velocity_rows(blocks):
    width = VELS // VBLOCKS
    number = (blocks[:, None] * width + jnp.arange(width, dtype=jnp.int32)[None, :]).reshape(-1).astype(jnp.int32)
    along_x = component(number // (VGRID * VGRID))
    along_y = component(number // VGRID % VGRID)
    along_z = component(number % VGRID)
    kinetic = along_x * along_x + along_y * along_y + along_z * along_z
    return jnp.stack([jnp.ones_like(along_x), along_x, along_y, along_z, kinetic])

def advect(padded, courant):
    length = padded.shape[0] - 4
    magnitude = jnp.abs(courant)
    lower = padded[0:length + 1]
    centre = padded[1:length + 2]
    upper = padded[2:length + 3]
    beyond = padded[3:length + 4]
    upwind = (1.0 - magnitude) / 2.0
    curved = (1.0 - magnitude * magnitude) / 6.0
    forward = centre + upwind * (upper - centre) - curved * (upper - 2.0 * centre + lower)
    backward = upper + upwind * (centre - upper) - curved * (centre - 2.0 * upper + beyond)
    flux = courant * jnp.where(courant >= 0.0, forward, backward)
    return padded[2:length + 2] - (flux[1:] - flux[:-1])

def project(fstar, collision, moments, energy_sum, restitution, basis):
    total, cross, quartic, square = grid_moments()
    sink = -SINK_RATE * (1.0 - restitution * restitution) * energy_sum
    excess = moments[4] - sink
    determinant = total * quartic - cross * cross
    mass_mult = (quartic * moments[0] - cross * excess) / determinant
    energy_mult = (total * excess - cross * moments[0]) / determinant
    weights = jnp.stack([mass_mult, moments[1] / square, moments[2] / square, moments[3] / square, energy_mult])
    correction = lax.dot_general(weights, basis, (((0,), (0,)), ((), ())), precision=lax.Precision.HIGHEST)
    return fstar + (collision - correction)

def collide(fstar, coder, w_latent, b_latent, restitution, basis):
    coarse = fstar.astype(jnp.bfloat16)
    encoded = jnp.dot(coarse, coder, preferred_element_type=jnp.float32)
    energy_sum = jnp.dot(fstar, basis[4], precision=lax.Precision.HIGHEST)
    active = jnp.tanh(jnp.dot(encoded.astype(jnp.bfloat16), w_latent, preferred_element_type=jnp.float32) + b_latent).astype(jnp.bfloat16)
    collision = math.sqrt(VELS / LATENT) * lax.dot_general(active, coder, (((1,), (1,)), ((), ())), preferred_element_type=jnp.float32)
    moments = lax.dot_general(basis, collision, (((1,), (1,)), ((), ())), precision=lax.Precision.HIGHEST)
    return project(fstar, collision, moments, energy_sum, restitution, basis)

def reference(density, coder, w_latent, b_latent, restitution, inflow, flags, blocks):
    basis = velocity_rows(blocks)
    courant = COURANT * basis[1]
    block_count = CELLS // C_DEV
    state = density.astype(jnp.float32)
    open_left = (flags == 1)[:, None, None]
    open_right = (jnp.concatenate([flags[1:], flags[:1]]) == 1)[:, None, None]
    for section_index in range(STEPS):
        grouped = state.reshape(block_count, C_DEV, VELS)
        before = jnp.concatenate([grouped[-1:, -2:], grouped[:-1, -2:]], 0)
        after_rows = jnp.concatenate([grouped[1:, :2], grouped[:1, :2]], 0)
        before = jnp.where(open_left, before, inflow[None, None, :])
        after_rows = jnp.where(open_right, after_rows, inflow[None, None, :])

        def one_block(members):
            block_cells, lead_rows, tail_rows, restit_rows = members
            padded = jnp.concatenate([lead_rows, block_cells, tail_rows], 0)
            return collide(advect(padded, courant), coder, w_latent, b_latent, restit_rows, basis)
        state = lax.map(one_block, (grouped, before, after_rows, restitution.reshape(block_count, C_DEV))).reshape(CELLS, VELS)
    return state.astype(jnp.bfloat16)
```

```python
import functools
import math

import jax
import jax.numpy as jnp
import numpy as np
from jax import lax
from jax.experimental import pallas as pl
from jax.experimental.pallas import tpu as pltpu
from jax.sharding import PartitionSpec as P

VGRID = 48
LATENT = 512
VBLOCKS = 96
STEPS = 2
VELS = 110592
WIDTH = VELS // VBLOCKS
LANES = 128
HALO = 4
SINK_RATE = 0.5
COURANT = 0.9
SCALE = math.sqrt(VELS / LATENT)
F32 = jnp.float32
BF16 = jnp.bfloat16


def grid_moments():
    centres = (2.0 * np.arange(VGRID) + 1.0 - VGRID) / VGRID
    second = float(np.sum(centres**2))
    fourth = float(np.sum(centres**4))
    number = float(VGRID)
    total = number**3
    cross = 3.0 * number * number * second
    quartic = 3.0 * number * number * fourth + 6.0 * number * second * second
    square = number * number * second
    return (total, cross, quartic, square)


def patterns():
    number = np.arange(WIDTH)
    rows = np.zeros((8, WIDTH), np.float32)
    for parity in range(2):
        rows[parity] = 2 * ((parity * WIDTH + number) // VGRID % VGRID) + 1 - VGRID
    rows[2] = 2 * (number % VGRID) + 1 - VGRID
    return rows


def taps(block):
    along = 2 * (block * WIDTH // (VGRID * VGRID)) + 1 - VGRID
    sign = jnp.where(along >= 0, 1, -1)
    along = along.astype(F32)
    a = jnp.abs(along) * (COURANT / VGRID)
    upwind = (1.0 - a) * 0.5
    curved = (1.0 - a * a) * (1.0 / 6.0)
    far = -a * curved
    behind = a * (1.0 - upwind + 3.0 * curved)
    here = 1.0 - a * (1.0 - 2.0 * upwind + 3.0 * curved)
    ahead = -a * (upwind - curved)
    return along, sign, (far, behind, here, ahead)


def stencil(ref, tile, first, count, sign, weights):
    far, behind, here, ahead = weights
    at = lambda shift: ref[tile, pl.ds(first + shift, count), :]
    return (
        far * at(-2 * sign) + behind * at(-sign) + here * at(0) + ahead * at(sign)
    )


def fill(pad, tile, lanes, density, left, right, inflow, open_left, open_right):
    cells = density.shape[0]
    ghost = inflow[:, lanes]
    pad[tile, 8 : 8 + cells, :] = density[:, lanes].astype(F32)
    pad[tile, 8 - HALO : 8, :] = jnp.where(open_left, left[:, lanes].astype(F32), ghost)
    pad[tile, 8 + cells : 8 + cells + HALO, :] = jnp.where(
        open_right, right[:, lanes].astype(F32), ghost
    )


def energy_row(total, rows):
    column = jnp.sum(total, axis=1, keepdims=True) * (1.0 / (VGRID * VGRID))
    row = lax.broadcasted_iota(jnp.int32, (rows, LANES), 0)
    lane = lax.broadcasted_iota(jnp.int32, (rows, LANES), 1)
    return jnp.sum(jnp.where(row == lane, column, 0.0), axis=0, keepdims=True)


def pattern_rows(pats, parity, lanes):
    y = jnp.where(parity == 0, pats[0:1, lanes], pats[1:2, lanes])
    return y, pats[2:3, lanes]


def first_kernel(
    nb, blocks, open_sides, density, left, right, inflow, coder, pats,
    sums, extra, pad, coarse, energy,
):
    step = pl.program_id(0)
    cells = density.shape[0]
    rows = cells + 2 * HALO
    tiles = WIDTH // LANES

    @pl.when(step == 0)
    def _():
        sums[...] = jnp.zeros_like(sums)
        energy[...] = jnp.zeros_like(energy)
        pad[...] = jnp.zeros_like(pad)

    open_left = open_sides[0] == 1
    open_right = open_sides[1] == 1
    kind = lax.broadcasted_iota(jnp.int32, (8, LANES), 0)
    for k in range(nb):
        block = blocks[step * nb + k]
        along, sign, weights = taps(block)
        parity = lax.rem(block, 2)
        total = energy[...]
        for t in range(tiles):
            lanes = slice(k * WIDTH + t * LANES, k * WIDTH + (t + 1) * LANES)
            tile = k * tiles + t
            fill(pad, tile, lanes, density, left, right, inflow, open_left, open_right)
            fstar = stencil(pad, tile, 8 - HALO, rows, sign, weights)
            y, z = pattern_rows(pats, parity, slice(t * LANES, (t + 1) * LANES))
            e = along * along + (y * y + z * z)
            total = total + fstar * e
            high = e.astype(BF16).astype(F32)
            basis = jnp.where(kind == 0, 1.0, 0.0)
            basis = jnp.where(kind == 1, along, basis)
            basis = jnp.where(kind == 2, y, basis)
            basis = jnp.where(kind == 3, z, basis)
            basis = jnp.where(kind == 4, high, basis)
            basis = jnp.where(kind == 5, e - high, basis)
            coarse[:, lanes] = jnp.concatenate([fstar, basis], 0).astype(BF16)
        energy[...] = total
    sums[...] += jnp.dot(coarse[...], coder[...], preferred_element_type=F32)

    @pl.when(step == pl.num_programs(0) - 1)
    def _():
        extra[0:1, :] = energy_row(energy[...], rows)


def prologue(active, moment_rows, energy, restitution, pats, consts, bands):
    total, cross, quartic, square = grid_moments()
    determinant = total * quartic - cross * cross
    rows = restitution.shape[0]
    inverse = 1.0 / VGRID
    act = active[0:rows, :].astype(F32)
    dots = [
        SCALE * jnp.sum(act * moment_rows[k : k + 1, :], axis=1, keepdims=True) for k in range(6)
    ]
    row = lax.broadcasted_iota(jnp.int32, (rows, LANES), 0)
    lane = lax.broadcasted_iota(jnp.int32, (rows, LANES), 1)
    energy_sum = jnp.sum(jnp.where(row == lane, energy[0:1, :], 0.0), axis=1, keepdims=True)
    r = restitution[...]
    sink = -SINK_RATE * (1.0 - r * r) * energy_sum
    excess = (dots[4] + dots[5]) * (inverse * inverse) - sink
    mass = (quartic * dots[0] - cross * excess) / determinant
    power = (total * excess - cross * dots[0]) / determinant * (inverse * inverse)
    slopes = [dots[k] * (inverse * inverse / square) for k in (1, 2, 3)]
    spread = lambda column: jnp.broadcast_to(column, (rows, LANES))
    consts[0] = spread(mass)
    consts[1] = spread(slopes[0])
    consts[2] = spread(power)
    power, second, third = spread(power), spread(slopes[1]), spread(slopes[2])
    for parity in range(2):
        for t in range(WIDTH // LANES):
            lanes = slice(t * LANES, (t + 1) * LANES)
            y, z = pats[parity : parity + 1, lanes], pats[2:3, lanes]
            bands[parity, t] = second * y + third * z + power * (y * y + z * z)


def second_kernel(
    nb, blocks, open_sides, density, left, right, inflow, coder, pats,
    active, moment_rows, energy_in, restitution,
    coarse, sums, extra, pad, state, decoded, energy, consts, bands,
):
    step = pl.program_id(0)
    cells = density.shape[0]
    rows = cells + 2 * HALO
    tiles = WIDTH // LANES

    @pl.when(step == 0)
    def _():
        sums[...] = jnp.zeros_like(sums)
        energy[...] = jnp.zeros_like(energy)
        pad[...] = jnp.zeros_like(pad)
        prologue(active, moment_rows, energy_in, restitution, pats, consts, bands)

    open_left = open_sides[0] == 1
    open_right = open_sides[1] == 1
    decoded[...] = lax.dot_general(
        active[...], coder[...], (((1,), (1,)), ((), ())), preferred_element_type=F32
    )
    for k in range(nb):
        block = blocks[step * nb + k]
        along, sign, weights = taps(block)
        parity = lax.rem(block, 2)
        level = consts[0] + along * consts[1] + (along * along) * consts[2]
        total = energy[...]
        for t in range(tiles):
            lanes = slice(k * WIDTH + t * LANES, k * WIDTH + (t + 1) * LANES)
            tile = k * tiles + t
            fill(pad, tile, lanes, density, left, right, inflow, open_left, open_right)
            fstar = stencil(pad, tile, 8 - HALO, rows, sign, weights)
            full = fstar + (SCALE * decoded[0:rows, lanes] - (level + bands[parity, t]))
            state[tile, :, :] = full
            ghost = jnp.broadcast_to(inflow[:, lanes], (HALO, LANES))

            @pl.when(jnp.logical_not(open_left))
            def _():
                state[tile, 0:HALO, :] = ghost

            @pl.when(jnp.logical_not(open_right))
            def _():
                state[tile, HALO + cells : rows, :] = ghost

            again = stencil(state, tile, HALO, cells, sign, weights)
            y, z = pattern_rows(pats, parity, slice(t * LANES, (t + 1) * LANES))
            total = total + again * (along * along + (y * y + z * z))
            coarse[:, lanes] = again.astype(BF16)
        energy[...] = total
    sums[...] += jnp.dot(coarse[...], coder[...], preferred_element_type=F32)

    @pl.when(step == pl.num_programs(0) - 1)
    def _():
        extra[0:1, :] = energy_row(energy[...], cells)


def third_kernel(
    nb, blocks, coarse, coder, pats, active, moment_rows, energy_in, restitution,
    out, decoded, consts, bands,
):
    step = pl.program_id(0)
    tiles = WIDTH // LANES

    @pl.when(step == 0)
    def _():
        prologue(active, moment_rows, energy_in, restitution, pats, consts, bands)

    decoded[...] = lax.dot_general(
        active[...], coder[...], (((1,), (1,)), ((), ())), preferred_element_type=F32
    )
    for k in range(nb):
        block = blocks[step * nb + k]
        along = (2 * (block * WIDTH // (VGRID * VGRID)) + 1 - VGRID).astype(F32)
        parity = lax.rem(block, 2)
        level = consts[0] + along * consts[1] + (along * along) * consts[2]
        for t in range(tiles):
            lanes = slice(k * WIDTH + t * LANES, k * WIDTH + (t + 1) * LANES)
            full = coarse[:, lanes].astype(F32) + (
                SCALE * decoded[:, lanes] - (level + bands[parity, t])
            )
            out[:, lanes] = full.astype(BF16)


def shifted(array, axes, count, shift):
    return lax.ppermute(array, axes, [(i, (i + shift) % count) for i in range(count)])


def latent_layer(encoded, w_latent, b_latent):
    mixed = jnp.dot(encoded.astype(BF16), w_latent, preferred_element_type=F32)
    return jnp.tanh(mixed + b_latent).astype(BF16)


def body(density, coder, w_latent, b_latent, restitution, inflow, flags, blocks):
    cells, vels = density.shape
    count = blocks.shape[0]
    nb = 2 if count % 2 == 0 else 1
    steps = count // nb
    tile = nb * WIDTH
    tiles = tile // LANES
    rows = cells + 2 * HALO
    ring = ("cell", "sub")
    sub_count = lax.axis_size("sub")
    ring_count = lax.axis_size("cell") * sub_count
    position = lax.axis_index("cell") * sub_count + lax.axis_index("sub")
    open_left = lax.dynamic_index_in_dim(flags, position, 0, keepdims=False)
    open_right = lax.dynamic_index_in_dim(flags, (position + 1) % ring_count, 0, keepdims=False)
    open_sides = jnp.stack([open_left, open_right])

    left = shifted(density[cells - HALO :], ring, ring_count, 1)
    right = shifted(density[:HALO], ring, ring_count, -1)
    left_r = shifted(restitution[cells - HALO :], ring, ring_count, 1)
    right_r = shifted(restitution[:HALO], ring, ring_count, -1)
    wide_r = jnp.concatenate([left_r, restitution, right_r])[:, None]
    pats = jnp.asarray(patterns())
    inflow = inflow[None, :]

    column = lambda height: pl.BlockSpec((height, tile), lambda i, *_: (0, i))
    whole = lambda *shape: pl.BlockSpec(shape, lambda i, *_: (0,) * len(shape))
    coder_spec = pl.BlockSpec((tile, LATENT), lambda i, *_: (i, 0))
    shape = jax.ShapeDtypeStruct
    params = pltpu.CompilerParams(
        dimension_semantics=("arbitrary",), vmem_limit_bytes=40 * 1024 * 1024
    )

    sums, extra = pl.pallas_call(
        functools.partial(first_kernel, nb),
        out_shape=(shape((rows + 8, LATENT), F32), shape((8, LANES), F32)),
        grid_spec=pltpu.PrefetchScalarGridSpec(
            num_scalar_prefetch=2,
            grid=(steps,),
            in_specs=[
                column(cells), column(HALO), column(HALO), column(1), coder_spec, whole(8, WIDTH),
            ],
            out_specs=(whole(rows + 8, LATENT), whole(8, LANES)),
            scratch_shapes=[
                pltpu.VMEM((tiles, rows + 8, LANES), F32),
                pltpu.VMEM((rows + 8, tile), BF16),
                pltpu.VMEM((rows, LANES), F32),
            ],
        ),
        compiler_params=params,
        name="first",
    )(blocks, open_sides, density, left, right, inflow, coder, pats)

    def exchange(sums, extra):
        sums, energy = lax.psum((sums, extra), "vel")
        return sums, energy

    sums, energy = exchange(sums, extra)
    moment_rows = sums[rows:]
    active = latent_layer(sums, w_latent, b_latent)

    coarse, sums, extra = pl.pallas_call(
        functools.partial(second_kernel, nb),
        out_shape=(
            shape((cells, vels), BF16), shape((cells, LATENT), F32), shape((8, LANES), F32),
        ),
        grid_spec=pltpu.PrefetchScalarGridSpec(
            num_scalar_prefetch=2,
            grid=(steps,),
            in_specs=[
                column(cells), column(HALO), column(HALO), column(1), coder_spec, whole(8, WIDTH),
                whole(rows + 8, LATENT), whole(8, LATENT), whole(8, LANES), whole(rows, 1),
            ],
            out_specs=(column(cells), whole(cells, LATENT), whole(8, LANES)),
            scratch_shapes=[
                pltpu.VMEM((tiles, rows + 8, LANES), F32),
                pltpu.VMEM((tiles, rows, LANES), F32),
                pltpu.VMEM((rows + 8, tile), F32),
                pltpu.VMEM((cells, LANES), F32),
                pltpu.VMEM((3, rows, LANES), F32),
                pltpu.VMEM((2, WIDTH // LANES, rows, LANES), F32),
            ],
        ),
        compiler_params=params,
        name="second",
    )(
        blocks, open_sides, density, left, right, inflow, coder, pats,
        active, moment_rows, energy, wide_r,
    )

    sums, energy = exchange(sums, extra)
    active = latent_layer(sums, w_latent, b_latent)

    return pl.pallas_call(
        functools.partial(third_kernel, nb),
        out_shape=shape((cells, vels), BF16),
        grid_spec=pltpu.PrefetchScalarGridSpec(
            num_scalar_prefetch=1,
            grid=(steps,),
            in_specs=[
                column(cells), coder_spec, whole(8, WIDTH),
                whole(cells, LATENT), whole(8, LATENT), whole(8, LANES), whole(cells, 1),
            ],
            out_specs=column(cells),
            scratch_shapes=[
                pltpu.VMEM((cells, tile), F32),
                pltpu.VMEM((3, cells, LANES), F32),
                pltpu.VMEM((2, WIDTH // LANES, cells, LANES), F32),
            ],
        ),
        compiler_params=params,
        name="third",
    )(blocks, coarse, coder, pats, active, moment_rows, energy, restitution[:, None])


def solution(mesh):
    return jax.shard_map(
        body,
        mesh=mesh,
        in_specs=(
            P(("groups", "cell", "sub"), "vel"),
            P("vel", None),
            P(),
            P(),
            P(("groups", "cell", "sub")),
            P(("groups", "vel")),
            P("groups"),
            P(("groups", "vel")),
        ),
        out_specs=P(("groups", "cell", "sub"), "vel"),
        check_vma=False,
    )
```

```python
import functools
import math

import jax
import jax.numpy as jnp
import numpy as np
from jax import lax
from jax.experimental import pallas as pl
from jax.experimental.pallas import tpu as pltpu
from jax.sharding import PartitionSpec as P

VGRID = 48
LATENT = 512
VBLOCKS = 96
STEPS = 2
VELS = 110592
WIDTH = VELS // VBLOCKS
LANES = 128
HALO = 4
SINK_RATE = 0.5
COURANT = 0.9
SCALE = math.sqrt(VELS / LATENT)
F32 = jnp.float32
BF16 = jnp.bfloat16


def grid_moments():
    centres = (2.0 * np.arange(VGRID) + 1.0 - VGRID) / VGRID
    second = float(np.sum(centres**2))
    fourth = float(np.sum(centres**4))
    number = float(VGRID)
    total = number**3
    cross = 3.0 * number * number * second
    quartic = 3.0 * number * number * fourth + 6.0 * number * second * second
    square = number * number * second
    return (total, cross, quartic, square)


def moment_pattern(pats):
    number = lax.broadcasted_iota(jnp.int32, (1, WIDTH), 1).astype(F32)
    along_y = jnp.floor((number + 0.5) * (1.0 / VGRID))
    along_z = number - VGRID * along_y
    first = 2.0 * along_y + (1 - VGRID)
    pats[0:1, :] = first
    pats[1:2, :] = first + (2 * WIDTH // VGRID)
    pats[2:3, :] = 2.0 * along_z + (1 - VGRID)


def taps(block):
    along = 2 * (block * WIDTH // (VGRID * VGRID)) + 1 - VGRID
    sign = jnp.where(along >= 0, 1, -1)
    along = along.astype(F32)
    a = jnp.abs(along) * (COURANT / VGRID)
    upwind = (1.0 - a) * 0.5
    curved = (1.0 - a * a) * (1.0 / 6.0)
    far = -a * curved
    behind = a * (1.0 - upwind + 3.0 * curved)
    here = 1.0 - a * (1.0 - 2.0 * upwind + 3.0 * curved)
    ahead = -a * (upwind - curved)
    return along, sign, (far, behind, here, ahead)


def stencil(ref, tile, first, count, sign, weights):
    far, behind, here, ahead = weights
    at = lambda shift: ref[tile, pl.ds(first + shift, count), :]
    return (
        far * at(-2 * sign) + behind * at(-sign) + here * at(0) + ahead * at(sign)
    )


def fill(pad, tile, lanes, far_lanes, density, left, right, inflow, open_left, open_right):
    cells = density.shape[0]
    ghost = inflow[:, far_lanes]
    pad[tile, 8 : 8 + cells, :] = density[:, lanes].astype(F32)
    pad[tile, 8 - HALO : 8, :] = jnp.where(open_left, left[:, far_lanes].astype(F32), ghost)
    pad[tile, 8 + cells : 8 + cells + HALO, :] = jnp.where(
        open_right, right[:, far_lanes].astype(F32), ghost
    )


def energy_row(total, rows):
    column = jnp.sum(total, axis=1, keepdims=True) * (1.0 / (VGRID * VGRID))
    row = lax.broadcasted_iota(jnp.int32, (rows, LANES), 0)
    lane = lax.broadcasted_iota(jnp.int32, (rows, LANES), 1)
    return jnp.sum(jnp.where(row == lane, column, 0.0), axis=0, keepdims=True)


def pattern_rows(pats, parity, lanes):
    y = jnp.where(parity == 0, pats[0:1, lanes], pats[1:2, lanes])
    return y, pats[2:3, lanes]


def sides(flags):
    sub_count = lax.axis_size("sub")
    count = lax.axis_size("cell") * sub_count
    position = lax.axis_index("cell") * sub_count + lax.axis_index("sub")
    return flags[position] == 1, flags[lax.rem(position + 1, count)] == 1


class Stream:
    def __init__(self, source, buffers, sems, tile, axis, inward=True):
        self.source, self.buffers, self.sems = source, buffers, sems
        self.tile, self.axis, self.inward = tile, axis, inward
        self.count = source.shape[axis] // tile
        self.slots = buffers.shape[0]

    def copy(self, i):
        slot = lax.rem(i, self.slots)
        span = pl.ds(pl.multiple_of(i * self.tile, LANES), self.tile)
        far = self.source.at[span, :] if self.axis == 0 else self.source.at[:, span]
        near = self.buffers.at[slot]
        source, target = (far, near) if self.inward else (near, far)
        return pltpu.make_async_copy(source, target, self.sems.at[slot])

    def begin(self, ahead):
        for i in range(min(ahead, self.count)):
            self.copy(i).start()

    def start(self, i):
        if isinstance(i, int):
            if i < self.count:
                self.copy(i).start()
        else:

            @pl.when(i < self.count)
            def _():
                self.copy(i).start()

    def wait(self, i):
        self.copy(i).wait()

    def at(self, i):
        return self.buffers.at[lax.rem(i, self.slots)]


def paired(first, last, step):
    pairs = (last - first) // 2
    if pairs > 1:

        def trip(j, carry):
            step(first + 2 * j, first % 2)
            step(first + 2 * j + 1, (first + 1) % 2)
            return carry

        lax.fori_loop(0, pairs, trip, 0)
        first = first + 2 * pairs
    for i in range(first, last):
        step(i, i % 2)


def scatter_rows(messages, sums, chunk, extra):
    count = len(messages)
    me = lax.axis_index("vel")
    for s in range(count):
        for k in range(count):

            @pl.when(lax.rem(me + s, count) == k)
            def _():
                messages[s][0:chunk, :] = sums[k * chunk : (k + 1) * chunk, :]

        for row, value in extra:
            messages[s][row : row + value.shape[0], 0 : value.shape[1]] = value


def gather_rows(wide, parts, chunk):
    count = len(parts)
    me = lax.axis_index("vel")
    for s in range(count):
        for k in range(count):

            @pl.when(lax.rem(me - s + count, count) == k)
            def _():
                wide[k * chunk : (k + 1) * chunk, :] = parts[s][0:chunk, :].astype(F32)


def first_kernel(shards, nb, blocks, flags, density, left, right, inflow, coder, *refs):
    messages = refs[:shards]
    pad, coarse_a, coarse_b, energy, pats, sums, tiles_c, sem_c, tiles_d, sem_d = refs[shards:]
    cells = density.shape[0]
    rows = cells + 2 * HALO
    width = nb * WIDTH
    tiles = WIDTH // LANES
    coders = Stream(coder, tiles_c, sem_c, width, 0)
    cells_in = Stream(density, tiles_d, sem_d, width, 1)
    ahead_c, ahead_d = coders.slots - 1, cells_in.slots
    coders.begin(ahead_c)
    cells_in.begin(ahead_d)
    steps = coders.count
    coarse = (coarse_a, coarse_b)

    moment_pattern(pats)
    sums[...] = jnp.zeros_like(sums)
    energy[...] = jnp.zeros_like(energy)
    pad[...] = jnp.zeros_like(pad)
    open_left, open_right = sides(flags)
    kind = lax.broadcasted_iota(jnp.int32, (8, LANES), 0)

    def transport(i, par):
        source = cells_in.at(i)
        for k in range(nb):
            block = blocks[i * nb + k]
            along, sign, weights = taps(block)
            parity = lax.rem(block, 2)
            total = energy[...]
            for t in range(tiles):
                tile = k * tiles + t
                lanes = slice(tile * LANES, (tile + 1) * LANES)
                far = pl.ds(pl.multiple_of(i * width + tile * LANES, LANES), LANES)
                fill(pad, tile, lanes, far, source, left, right, inflow, open_left, open_right)
                fstar = stencil(pad, tile, 8 - HALO, rows, sign, weights)
                y, z = pattern_rows(pats, parity, slice(t * LANES, (t + 1) * LANES))
                e = along * along + (y * y + z * z)
                total = total + fstar * e
                high = e.astype(BF16).astype(F32)
                basis = jnp.where(kind == 0, 1.0, 0.0)
                basis = jnp.where(kind == 1, along, basis)
                basis = jnp.where(kind == 2, y, basis)
                basis = jnp.where(kind == 3, z, basis)
                basis = jnp.where(kind == 4, high, basis)
                basis = jnp.where(kind == 5, e - high, basis)
                coarse[par][:, lanes] = jnp.concatenate([fstar, basis], 0).astype(BF16)
            energy[...] = total

    def encode(i, par):
        sums[...] += jnp.dot(coarse[par][...], coders.at(i)[...], preferred_element_type=F32)

    def step(i, par):
        cells_in.wait(i)
        coders.wait(i)
        coders.start(i + ahead_c - 1)
        encode(i - 1, 1 - par)
        transport(i, par)
        cells_in.start(i + ahead_d)

    cells_in.wait(0)
    transport(0, 0)
    cells_in.start(ahead_d)
    coders.wait(0)
    paired(1, steps, step)
    encode(steps - 1, (steps - 1) % 2)

    moments = sums[rows : rows + 4, :]
    last = sums[rows + 4 : rows + 5, :] + sums[rows + 5 : rows + 6, :]
    chunk = rows // shards
    scatter_rows(
        messages, sums, chunk,
        ((chunk, moments), (chunk + 4, last), (chunk + 5, energy_row(energy[...], rows))),
    )


def project(act, moments, energy, restitution, pats, consts, bands):
    total, cross, quartic, square = grid_moments()
    determinant = total * quartic - cross * cross
    rows = restitution.shape[0]
    inverse = 1.0 / VGRID
    dots = [
        SCALE * jnp.sum(act * moments[k : k + 1, :], axis=1, keepdims=True) for k in range(5)
    ]
    row = lax.broadcasted_iota(jnp.int32, (rows, LANES), 0)
    lane = lax.broadcasted_iota(jnp.int32, (rows, LANES), 1)
    energy_sum = jnp.sum(jnp.where(row == lane, energy, 0.0), axis=1, keepdims=True)
    sink = -SINK_RATE * (1.0 - restitution * restitution) * energy_sum
    excess = dots[4] * (inverse * inverse) - sink
    mass = (quartic * dots[0] - cross * excess) / determinant
    power = (total * excess - cross * dots[0]) / determinant * (inverse * inverse)
    slopes = [dots[k] * (inverse * inverse / square) for k in (1, 2, 3)]
    spread = lambda column: jnp.broadcast_to(column, (rows, LANES))
    consts[0] = spread(mass)
    consts[1] = spread(slopes[0])
    consts[2] = spread(power)
    power, second, third = spread(power), spread(slopes[1]), spread(slopes[2])
    for parity in range(2):
        for t in range(WIDTH // LANES):
            lanes = slice(t * LANES, (t + 1) * LANES)
            y, z = pats[parity : parity + 1, lanes], pats[2:3, lanes]
            bands[parity, t] = second * y + third * z + power * (y * y + z * z)


def diagonal(row, first, rows):
    shape = (rows, row.shape[1])
    place = lax.broadcasted_iota(jnp.int32, shape, 0) - first
    lane = lax.broadcasted_iota(jnp.int32, shape, 1)
    return jnp.sum(jnp.where(place == lane, row, 0.0), axis=1, keepdims=True)


def second_kernel(
    shards, nb, blocks, flags, density, left, right, inflow, coder, mine, restitution, *refs
):
    parts, refs = refs[:shards], refs[shards:]
    out, messages, refs = refs[0], refs[1 : 1 + shards], refs[1 + shards :]
    (
        pad, state, decoded_a, decoded_b, coarse, energy, pats, sums, wide, active, consts, bands,
        tiles_c, sem_c, tiles_d, sem_d, sem_o,
    ) = refs
    cells = density.shape[0]
    rows = cells + 2 * HALO
    width = nb * WIDTH
    tiles = WIDTH // LANES
    coders = Stream(coder, tiles_c, sem_c, width, 0)
    cells_in = Stream(density, tiles_d, sem_d, width, 1)
    cells_out = Stream(out, coarse, sem_o, width, 1, inward=False)
    ahead_c, ahead_d = coders.slots - 2, cells_in.slots
    coders.begin(ahead_c)
    cells_in.begin(ahead_d)
    steps = coders.count
    decoded = (decoded_a, decoded_b)
    vels = density.shape[1]

    moment_pattern(pats)
    sums[...] = jnp.zeros_like(sums)
    energy[...] = jnp.zeros_like(energy)
    pad[...] = jnp.zeros_like(pad)
    open_left, open_right = sides(flags)
    chunk = rows // shards
    gather_rows(wide, parts, chunk)
    active[...] = jnp.zeros_like(active)
    active[0:rows, :] = wide[...].astype(BF16)
    ghosts = [jnp.sum(side[:, vels:].astype(F32), axis=1, keepdims=True) for side in (left, right)]
    r = diagonal(restitution[...], HALO, rows)
    state[0, 0:rows, :] = jnp.broadcast_to(r, (rows, LANES))
    state[0, 0:HALO, :] = jnp.broadcast_to(ghosts[0], (HALO, LANES))
    state[0, HALO + cells : rows, :] = jnp.broadcast_to(ghosts[1], (HALO, LANES))
    project(
        wide[...], mine[chunk : chunk + 5, :], mine[chunk + 5 : chunk + 6, 0:LANES],
        state[0, :, 0:1], pats, consts, bands,
    )
    place = lax.broadcasted_iota(jnp.int32, (8, LANES), 0)
    cut_top = jnp.logical_and(place < HALO, jnp.logical_not(open_left))
    cut_bottom = jnp.logical_and(place >= 8 - HALO, jnp.logical_not(open_right))

    def decode(i, par):
        decoded[par][...] = lax.dot_general(
            active[...], coders.at(i)[...], (((1,), (1,)), ((), ())), preferred_element_type=F32
        )

    def transport(i, par):
        source = cells_in.at(i)
        target = cells_out.at(i)
        for k in range(nb):
            block = blocks[i * nb + k]
            along, sign, weights = taps(block)
            parity = lax.rem(block, 2)
            level = consts[0] + along * consts[1] + (along * along) * consts[2]
            total = energy[...]
            for t in range(tiles):
                tile = k * tiles + t
                lanes = slice(tile * LANES, (tile + 1) * LANES)
                far = pl.ds(pl.multiple_of(i * width + tile * LANES, LANES), LANES)
                fill(pad, tile, lanes, far, source, left, right, inflow, open_left, open_right)
                fstar = stencil(pad, tile, 8 - HALO, rows, sign, weights)
                full = fstar + (
                    SCALE * decoded[par][0:rows, lanes] - (level + bands[parity, t])
                )
                ghost = inflow[:, far]
                state[tile, 0:8, :] = jnp.where(cut_top, ghost, full[0:8])
                state[tile, 8 : rows - 8, :] = full[8 : rows - 8]
                state[tile, rows - 8 : rows, :] = jnp.where(cut_bottom, ghost, full[rows - 8 :])
                again = stencil(state, tile, HALO, cells, sign, weights)
                y, z = pattern_rows(pats, parity, slice(t * LANES, (t + 1) * LANES))
                total = total + again * (along * along + (y * y + z * z))
                target[:, lanes] = again.astype(BF16)
            energy[...] = total

    def encode(i, par):
        sums[...] += jnp.dot(
            cells_out.at(i)[...], coders.at(i)[...], preferred_element_type=F32
        )

    def step(i, par):
        cells_in.wait(i)
        coders.wait(i + 1)
        coders.start(i + ahead_c)
        if isinstance(i, int):
            if i >= cells_out.slots:
                cells_out.wait(i - cells_out.slots)
        else:

            @pl.when(i >= cells_out.slots)
            def _():
                cells_out.wait(i - cells_out.slots)

        encode(i - 1, 1 - par)
        decode(i + 1, 1 - par)
        transport(i, par)
        cells_in.start(i + ahead_d)
        cells_out.start(i)

    coders.wait(0)
    decode(0, 0)
    cells_in.wait(0)
    coders.wait(1)
    coders.start(ahead_c)
    decode(1, 1)
    transport(0, 0)
    cells_in.start(ahead_d)
    cells_out.start(0)
    paired(1, steps - 1, step)
    last = steps - 1
    cells_in.wait(last)
    if last >= cells_out.slots:
        cells_out.wait(last - cells_out.slots)
    encode(last - 1, (last - 1) % 2)
    transport(last, last % 2)
    cells_out.start(last)
    encode(last, last % 2)
    chunk = cells // shards
    scatter_rows(messages, sums, chunk, ((rows // shards + 5, energy_row(energy[...], cells)),))
    for i in range(max(0, steps - cells_out.slots), steps):
        cells_out.wait(i)


def third_kernel(shards, nb, blocks, source, coder, mine, energies, restitution, *refs):
    parts, refs = refs[:shards], refs[shards:]
    (
        out, decoded_a, decoded_b, result, pats, wide, active, consts, bands,
        tiles_c, sem_c, tiles_d, sem_d, sem_o,
    ) = refs
    cells = source.shape[0]
    rows = cells + 2 * HALO
    width = nb * WIDTH
    tiles = WIDTH // LANES
    coders = Stream(coder, tiles_c, sem_c, width, 0)
    cells_in = Stream(source, tiles_d, sem_d, width, 1)
    cells_out = Stream(out, result, sem_o, width, 1, inward=False)
    ahead_c, ahead_d = coders.slots - 1, cells_in.slots
    coders.begin(ahead_c)
    cells_in.begin(ahead_d)
    steps = coders.count
    decoded = (decoded_a, decoded_b)

    moment_pattern(pats)
    gather_rows(wide, parts, cells // shards)
    active[...] = wide[...].astype(BF16)
    chunk = rows // shards
    project(
        wide[...], mine[chunk : chunk + 5, :], energies[chunk + 5 : chunk + 6, 0:LANES],
        diagonal(restitution[...], 0, cells), pats, consts, bands,
    )

    def decode(i, par):
        decoded[par][...] = lax.dot_general(
            active[...], coders.at(i)[...], (((1,), (1,)), ((), ())), preferred_element_type=F32
        )

    def finish(i, par):
        here = cells_in.at(i)
        target = cells_out.at(i)
        for k in range(nb):
            block = blocks[i * nb + k]
            along = (2 * (block * WIDTH // (VGRID * VGRID)) + 1 - VGRID).astype(F32)
            parity = lax.rem(block, 2)
            level = consts[0] + along * consts[1] + (along * along) * consts[2]
            for t in range(tiles):
                tile = k * tiles + t
                lanes = slice(tile * LANES, (tile + 1) * LANES)
                full = here[:, lanes].astype(F32) + (
                    SCALE * decoded[par][:, lanes] - (level + bands[parity, t])
                )
                target[:, lanes] = full.astype(BF16)

    def drain(i):
        if isinstance(i, int):
            if i >= cells_out.slots:
                cells_out.wait(i - cells_out.slots)
        else:

            @pl.when(i >= cells_out.slots)
            def _():
                cells_out.wait(i - cells_out.slots)

    def step(i, par):
        coders.wait(i)
        coders.start(i + ahead_c)
        cells_in.wait(i - 1)
        drain(i - 1)
        decode(i, par)
        finish(i - 1, 1 - par)
        cells_in.start(i - 1 + ahead_d)
        cells_out.start(i - 1)

    coders.wait(0)
    coders.start(ahead_c)
    decode(0, 0)
    paired(1, steps, step)
    last = steps - 1
    cells_in.wait(last)
    drain(last)
    finish(last, last % 2)
    cells_out.start(last)
    for i in range(max(0, steps - cells_out.slots), steps):
        cells_out.wait(i)


def shifted(array, axes, count, shift):
    return lax.ppermute(array, axes, [(i, (i + shift) % count) for i in range(count)])


def latent_layer(encoded, w_latent, b_latent):
    mixed = jnp.dot(encoded.astype(BF16), w_latent, preferred_element_type=F32)
    return jnp.tanh(mixed + b_latent).astype(BF16)


def pieces(values):
    first = lax.reduce_precision(values, 8, 7)
    second = lax.reduce_precision(values - first, 8, 7)
    third = values - first - second
    return jnp.stack([first, second, third], -1).astype(BF16)


def exchange(messages, w_latent, b_latent):
    count = len(messages)
    total = messages[0] if count > 1 else lax.psum(messages[0], "vel")
    for s in range(1, count):
        total = total + shifted(messages[s], "vel", count, s)
    own = latent_layer(total, w_latent, b_latent)
    return total, [own] + [shifted(own, "vel", count, s) for s in range(1, count)]


def body(density, coder, w_latent, b_latent, restitution, inflow, flags, blocks):
    cells, vels = density.shape
    count = blocks.shape[0]
    nb = 2 if count % 2 == 0 else 1
    width = nb * WIDTH
    tiles = width // LANES
    rows = cells + 2 * HALO
    ring = ("cell", "sub")
    ring_count = lax.axis_size("cell") * lax.axis_size("sub")
    shards = lax.axis_size("vel")
    if rows % shards or cells % shards or shards > 8:
        shards = 1

    def edge(part, r):
        extra = jnp.pad(pieces(r), ((0, 0), (0, LANES - 3)))
        return jnp.concatenate([part, extra], 1)

    left = shifted(edge(density[cells - HALO :], restitution[cells - HALO :]), ring, ring_count, 1)
    right = shifted(edge(density[:HALO], restitution[:HALO]), ring, ring_count, -1)
    inflow = inflow[None, :]
    restitution = restitution[None, :]

    shape = jax.ShapeDtypeStruct
    vmem = pl.BlockSpec(memory_space=pltpu.VMEM)
    smem = pl.BlockSpec(memory_space=pltpu.SMEM)
    hbm = pl.BlockSpec(memory_space=pl.ANY)
    params = pltpu.CompilerParams(vmem_limit_bytes=60 * 1024 * 1024)
    dma = pltpu.SemaphoreType.DMA
    message = shape((-(-(rows // shards + 6) // 8) * 8, LATENT), F32)

    messages = pl.pallas_call(
        functools.partial(first_kernel, shards, nb),
        out_shape=(message,) * shards,
        in_specs=[smem, smem, hbm, vmem, vmem, vmem, hbm],
        out_specs=(vmem,) * shards,
        scratch_shapes=[
            pltpu.VMEM((tiles, rows + 8, LANES), F32),
            pltpu.VMEM((rows + 8, width), BF16),
            pltpu.VMEM((rows + 8, width), BF16),
            pltpu.VMEM((rows, LANES), F32),
            pltpu.VMEM((8, WIDTH), F32),
            pltpu.VMEM((rows + 8, LATENT), F32),
            pltpu.VMEM((5, width, LATENT), BF16),
            dma((5,)),
            pltpu.VMEM((3, cells, width), BF16),
            dma((3,)),
        ],
        compiler_params=params,
        name="first",
    )(blocks, flags, density, left, right, inflow, coder)

    mine, parts = exchange(messages, w_latent, b_latent)

    coarse, *messages = pl.pallas_call(
        functools.partial(second_kernel, shards, nb),
        out_shape=(shape((cells, vels), BF16),) + (message,) * shards,
        in_specs=[smem, smem, hbm, vmem, vmem, vmem, hbm, vmem, vmem] + [vmem] * shards,
        out_specs=(hbm,) + (vmem,) * shards,
        scratch_shapes=[
            pltpu.VMEM((tiles, rows + 8, LANES), F32),
            pltpu.VMEM((tiles, rows, LANES), F32),
            pltpu.VMEM((rows + 8, width), F32),
            pltpu.VMEM((rows + 8, width), F32),
            pltpu.VMEM((2, cells, width), BF16),
            pltpu.VMEM((cells, LANES), F32),
            pltpu.VMEM((8, WIDTH), F32),
            pltpu.VMEM((cells, LATENT), F32),
            pltpu.VMEM((rows, LATENT), F32),
            pltpu.VMEM((rows + 8, LATENT), BF16),
            pltpu.VMEM((3, rows, LANES), F32),
            pltpu.VMEM((2, WIDTH // LANES, rows, LANES), F32),
            pltpu.VMEM((6, width, LATENT), BF16),
            dma((6,)),
            pltpu.VMEM((3, cells, width), BF16),
            dma((3,)),
            dma((2,)),
        ],
        compiler_params=params,
        name="second",
    )(blocks, flags, density, left, right, inflow, coder, mine, restitution, *parts)

    energies, parts = exchange(messages, w_latent, b_latent)

    return pl.pallas_call(
        functools.partial(third_kernel, shards, nb),
        out_shape=shape((cells, vels), BF16),
        in_specs=[smem, hbm, hbm, vmem, vmem, vmem] + [vmem] * shards,
        out_specs=hbm,
        scratch_shapes=[
            pltpu.VMEM((cells, width), F32),
            pltpu.VMEM((cells, width), F32),
            pltpu.VMEM((2, cells, width), BF16),
            pltpu.VMEM((8, WIDTH), F32),
            pltpu.VMEM((cells, LATENT), F32),
            pltpu.VMEM((cells, LATENT), BF16),
            pltpu.VMEM((3, cells, LANES), F32),
            pltpu.VMEM((2, WIDTH // LANES, cells, LANES), F32),
            pltpu.VMEM((5, width, LATENT), BF16),
            dma((5,)),
            pltpu.VMEM((3, cells, width), BF16),
            dma((3,)),
            dma((2,)),
        ],
        compiler_params=params,
        name="third",
    )(blocks, coarse, coder, mine, energies, restitution, *parts)


def solution(mesh):
    return jax.shard_map(
        body,
        mesh=mesh,
        in_specs=(
            P(("groups", "cell", "sub"), "vel"),
            P("vel", None),
            P(),
            P(),
            P(("groups", "cell", "sub")),
            P(("groups", "vel")),
            P("groups"),
            P(("groups", "vel")),
        ),
        out_specs=P(("groups", "cell", "sub"), "vel"),
        check_vma=False,
    )
```

```python
import functools
import math

import jax
import jax.numpy as jnp
import numpy as np
from jax import lax
from jax.experimental import pallas as pl
from jax.experimental.pallas import tpu as pltpu
from jax.sharding import PartitionSpec as P

VGRID = 48
LATENT = 512
VBLOCKS = 96
STEPS = 2
VELS = 110592
WIDTH = VELS // VBLOCKS
LANES = 128
HALO = 4
RING = 4
GROUP = 9
VMEM_MIB = 57
SINK_RATE = 0.5
COURANT = 0.9
SCALE = math.sqrt(VELS / LATENT)
F32 = jnp.float32
BF16 = jnp.bfloat16


def grid_moments():
    centres = (2.0 * np.arange(VGRID) + 1.0 - VGRID) / VGRID
    second = float(np.sum(centres**2))
    fourth = float(np.sum(centres**4))
    number = float(VGRID)
    total = number**3
    cross = 3.0 * number * number * second
    quartic = 3.0 * number * number * fourth + 6.0 * number * second * second
    square = number * number * second
    return (total, cross, quartic, square)


def moment_pattern(pats):
    number = lax.broadcasted_iota(jnp.int32, (1, WIDTH), 1).astype(F32)
    along_y = jnp.floor((number + 0.5) * (1.0 / VGRID))
    along_z = number - VGRID * along_y
    first = 2.0 * along_y + (1 - VGRID)
    pats[0:1, :] = first
    pats[1:2, :] = first + (2 * WIDTH // VGRID)
    pats[2:3, :] = 2.0 * along_z + (1 - VGRID)


def taps(block):
    along = 2 * (block * WIDTH // (VGRID * VGRID)) + 1 - VGRID
    sign = jnp.where(along >= 0, 1, -1)
    along = along.astype(F32)
    a = jnp.abs(along) * (COURANT / VGRID)
    upwind = (1.0 - a) * 0.5
    curved = (1.0 - a * a) * (1.0 / 6.0)
    far = -a * curved
    behind = a * (1.0 - upwind + 3.0 * curved)
    here = 1.0 - a * (1.0 - 2.0 * upwind + 3.0 * curved)
    ahead = -a * (upwind - curved)
    return along, sign, (far, behind, here, ahead)


def stencil(ref, tile, first, count, sign, weights):
    far, behind, here, ahead = weights
    at = lambda shift: ref[tile, pl.ds(first + shift, count), :]
    return (
        far * at(-2 * sign) + behind * at(-sign) + here * at(0) + ahead * at(sign)
    )


def fill(pad, tile, lanes, far_lanes, density, left, right, inflow, open_left, open_right):
    cells = density.shape[0]
    ghost = inflow[:, far_lanes]
    pad[tile, 8 : 8 + cells, :] = density[:, lanes].astype(F32)
    pad[tile, 8 - HALO : 8, :] = jnp.where(open_left, left[:, far_lanes].astype(F32), ghost)
    pad[tile, 8 + cells : 8 + cells + HALO, :] = jnp.where(
        open_right, right[:, far_lanes].astype(F32), ghost
    )


def energy_row(total, rows):
    column = jnp.sum(total, axis=1, keepdims=True) * (1.0 / (VGRID * VGRID))
    row = lax.broadcasted_iota(jnp.int32, (rows, LANES), 0)
    lane = lax.broadcasted_iota(jnp.int32, (rows, LANES), 1)
    return jnp.sum(jnp.where(row == lane, column, 0.0), axis=0, keepdims=True)


def pattern_rows(pats, parity, lanes):
    y = jnp.where(parity == 0, pats[0:1, lanes], pats[1:2, lanes])
    return y, pats[2:3, lanes]


def sides(flags):
    sub_count = lax.axis_size("sub")
    count = lax.axis_size("cell") * sub_count
    position = lax.axis_index("cell") * sub_count + lax.axis_index("sub")
    return flags[position] == 1, flags[lax.rem(position + 1, count)] == 1


class Stream:
    def __init__(self, source, buffers, sems, tile, axis, inward=True):
        self.source, self.buffers, self.sems = source, buffers, sems
        self.tile, self.axis, self.inward = tile, axis, inward
        self.count = source.shape[axis] // tile
        self.slots = buffers.shape[0]

    def copy(self, i, u):
        slot = u % self.slots
        span = pl.ds(pl.multiple_of(i * self.tile, LANES), self.tile)
        far = self.source.at[span, :] if self.axis == 0 else self.source.at[:, span]
        near = self.buffers.at[slot]
        source, target = (far, near) if self.inward else (near, far)
        return pltpu.make_async_copy(source, target, self.sems.at[slot])

    def begin(self, ahead):
        for i in range(min(ahead, self.count)):
            self.copy(i, i).start()

    def start(self, i, u):
        if isinstance(i, int):
            if i < self.count:
                self.copy(i, u).start()
        else:

            @pl.when(i < self.count)
            def _():
                self.copy(i, u).start()

    def wait(self, i, u):
        self.copy(i, u).wait()

    def drain(self, i, u):
        if isinstance(i, int):
            if i >= self.slots:
                self.wait(i - self.slots, u)
        else:

            @pl.when(i >= self.slots)
            def _():
                self.wait(i - self.slots, u)

    def at(self, u):
        return self.buffers.at[u % self.slots]


def unrolled(first, last, step):
    trips = (last - first) // RING
    if trips > 1:

        def trip(j, carry):
            for k in range(RING):
                step(first + RING * j + k, (first + k) % RING)
            return carry

        lax.fori_loop(0, trips, trip, 0)
        first = first + RING * trips
    for i in range(first, last):
        step(i, i % RING)


def put_parts(message, row_of, values, count, lane_step=0):
    height, width = values.shape
    for k in range(count):
        part = values.astype(BF16)
        values = values - part.astype(F32)
        for r in range(height):
            lanes = slice(k * lane_step, k * lane_step + width)
            message[row_of(k, r) : row_of(k, r) + 1, lanes] = part[r : r + 1]


def moment_row(rows, k, r):
    place = 5 * k + r
    return rows + place if place < 8 else rows - 2 + (place - 8)


def first_kernel(nb, blocks, flags, density, left, right, inflow, coder, message, *refs):
    pad, coarse_a, coarse_b, energy, pats, sums, tiles_c, sem_c, tiles_d, sem_d = refs
    cells = density.shape[0]
    rows = cells + 2 * HALO
    width = nb * WIDTH
    tiles = WIDTH // LANES
    coders = Stream(coder, tiles_c, sem_c, width, 0)
    cells_in = Stream(density, tiles_d, sem_d, width, 1)
    cells_in.begin(1)
    coders.begin(RING - 1)
    for i in range(1, min(RING - 1, cells_in.count)):
        cells_in.copy(i, i).start()
    steps = coders.count
    coarse = (coarse_a, coarse_b)

    moment_pattern(pats)
    sums[...] = jnp.zeros_like(sums)
    energy[...] = jnp.zeros_like(energy)
    pad[...] = jnp.zeros_like(pad)
    open_left, open_right = sides(flags)
    kind = lax.broadcasted_iota(jnp.int32, (8, LANES), 0)

    def transport(i, u):
        source = cells_in.at(u)
        for k in range(nb):
            block = blocks[i * nb + k]
            along, sign, weights = taps(block)
            parity = lax.rem(block, 2)
            total = energy[...]
            for t in range(tiles):
                tile = k * tiles + t
                lanes = slice(tile * LANES, (tile + 1) * LANES)
                far = pl.ds(pl.multiple_of(i * width + tile * LANES, LANES), LANES)
                fill(pad, tile, lanes, far, source, left, right, inflow, open_left, open_right)
                fstar = stencil(pad, tile, 8 - HALO, rows, sign, weights)
                y, z = pattern_rows(pats, parity, slice(t * LANES, (t + 1) * LANES))
                e = along * along + (y * y + z * z)
                total = total + fstar * e
                high = e.astype(BF16).astype(F32)
                basis = jnp.where(kind == 0, 1.0, 0.0)
                basis = jnp.where(kind == 1, along, basis)
                basis = jnp.where(kind == 2, y, basis)
                basis = jnp.where(kind == 3, z, basis)
                basis = jnp.where(kind == 4, high, basis)
                basis = jnp.where(kind == 5, e - high, basis)
                coarse[u % 2][:, lanes] = jnp.concatenate([fstar, basis], 0).astype(BF16)
            energy[...] = total

    def encode(u):
        sums[...] += jnp.dot(coarse[u % 2][...], coders.at(u)[...], preferred_element_type=F32)

    def step(i, u):
        cells_in.wait(i, u)
        coders.wait(i, u)
        coders.start(i + RING - 2, u + RING - 2)
        cells_in.start(i + RING - 2, u + RING - 2)
        encode(u + RING - 1)
        transport(i, u)

    cells_in.wait(0, 0)
    transport(0, 0)
    coders.wait(0, 0)
    unrolled(1, steps, step)
    encode(steps - 1)

    message[0:rows, :] = sums[0:rows, :].astype(BF16)
    last = sums[rows + 4 : rows + 5, :] + sums[rows + 5 : rows + 6, :]
    moments = jnp.concatenate([sums[rows : rows + 4, :], last], 0)
    put_parts(message, functools.partial(moment_row, rows), moments, 2)
    put_parts(message, lambda k, r: 0, energy_row(energy[...], rows), 3, LANES)


def project(act, moments, energy, restitution, pats, consts, bands):
    total, cross, quartic, square = grid_moments()
    determinant = total * quartic - cross * cross
    rows = restitution.shape[0]
    inverse = 1.0 / VGRID
    dots = [
        SCALE * jnp.sum(act * moments[k : k + 1, :], axis=1, keepdims=True) for k in range(5)
    ]
    row = lax.broadcasted_iota(jnp.int32, (rows, LANES), 0)
    lane = lax.broadcasted_iota(jnp.int32, (rows, LANES), 1)
    energy_sum = jnp.sum(jnp.where(row == lane, energy, 0.0), axis=1, keepdims=True)
    sink = -SINK_RATE * (1.0 - restitution * restitution) * energy_sum
    excess = dots[4] * (inverse * inverse) - sink
    mass = (quartic * dots[0] - cross * excess) / determinant
    power = (total * excess - cross * dots[0]) / determinant * (inverse * inverse)
    slopes = [dots[k] * (inverse * inverse / square) for k in (1, 2, 3)]
    spread = lambda column: jnp.broadcast_to(column, (rows, LANES))
    consts[0] = spread(mass)
    consts[1] = spread(slopes[0])
    consts[2] = spread(power)
    power, second, third = spread(power), spread(slopes[1]), spread(slopes[2])
    for parity in range(2):
        for t in range(WIDTH // LANES):
            lanes = slice(t * LANES, (t + 1) * LANES)
            y, z = pats[parity : parity + 1, lanes], pats[2:3, lanes]
            bands[parity, t] = second * y + third * z + power * (y * y + z * z)


def diagonal(row, first, rows):
    shape = (rows, row.shape[1])
    place = lax.broadcasted_iota(jnp.int32, shape, 0) - first
    lane = lax.broadcasted_iota(jnp.int32, shape, 1)
    return jnp.sum(jnp.where(place == lane, row, 0.0), axis=1, keepdims=True)


def collect(message, others, total):
    total[...] = message[...].astype(F32)
    for other in others:
        total[...] += other[...].astype(F32)


def energy_of(total, row):
    return sum(total[row : row + 1, k * LANES : (k + 1) * LANES] for k in range(3))


def latent_layer(total, w_latent, b_latent, active):
    mixed = jnp.dot(total[...].astype(BF16), w_latent[...], preferred_element_type=F32)
    active[...] = jnp.tanh(mixed + b_latent[...]).astype(BF16)


def diagonal(row, first, rows):
    shape = (rows, row.shape[1])
    place = lax.broadcasted_iota(jnp.int32, shape, 0) - first
    lane = lax.broadcasted_iota(jnp.int32, shape, 1)
    return jnp.sum(jnp.where(place == lane, row, 0.0), axis=1, keepdims=True)


def second_kernel(
    nb, peers, blocks, flags, density, left, right, inflow, coder, w_latent, b_latent,
    restitution, *refs
):
    parts, refs = refs[:peers], refs[peers:]
    (
        out, message, moments, pad, state, decoded_a, decoded_b, coarse, energy, pats, sums,
        total, active, consts, bands, weights_in, sem_w,
        tiles_c, sem_c, tiles_d, sem_d, sem_o,
    ) = refs
    cells = density.shape[0]
    rows = cells + 2 * HALO
    width = nb * WIDTH
    tiles = WIDTH // LANES
    load = pltpu.make_async_copy(w_latent, weights_in, sem_w)
    load.start()
    coders = Stream(coder, tiles_c, sem_c, width, 0)
    cells_in = Stream(density, tiles_d, sem_d, width, 1)
    cells_out = Stream(out, coarse, sem_o, width, 1, inward=False)
    coders.begin(RING - 1)
    cells_in.begin(RING - 1)
    steps = coders.count
    decoded = (decoded_a, decoded_b)
    vels = density.shape[1]

    collect(parts[0], parts[1:], total)
    moment_pattern(pats)
    sums[...] = jnp.zeros_like(sums)
    energy[...] = jnp.zeros_like(energy)
    pad[...] = jnp.zeros_like(pad)
    open_left, open_right = sides(flags)
    for r in range(5):
        at = [moment_row(rows, k, r) for k in range(2)]
        moments[r : r + 1, :] = total[at[0] : at[0] + 1, :] + total[at[1] : at[1] + 1, :]
    ghosts = [jnp.sum(side[:, vels:].astype(F32), axis=1, keepdims=True) for side in (left, right)]
    r = diagonal(restitution[...], HALO, rows)
    state[0, 0:rows, :] = jnp.broadcast_to(r, (rows, LANES))
    state[0, 0:HALO, :] = jnp.broadcast_to(ghosts[0], (HALO, LANES))
    state[0, HALO + cells : rows, :] = jnp.broadcast_to(ghosts[1], (HALO, LANES))
    load.wait()
    latent_layer(total, weights_in, b_latent, active)
    project(
        active[0:rows, :].astype(F32), moments, energy_of(total, 0), state[0, :, 0:1],
        pats, consts, bands,
    )
    place = lax.broadcasted_iota(jnp.int32, (8, LANES), 0)
    cut_top = jnp.logical_and(place < HALO, jnp.logical_not(open_left))
    cut_bottom = jnp.logical_and(place >= 8 - HALO, jnp.logical_not(open_right))

    def decode_part(u, tile, count):
        span = slice(tile * LANES, (tile + count) * LANES)
        decoded[u % 2][:, span] = lax.dot_general(
            active[...], coders.at(u)[span, :], (((1,), (1,)), ((), ())),
            preferred_element_type=F32,
        )

    def encode_part(u, tile, count):
        span = slice(tile * LANES, (tile + count) * LANES)
        sums[...] += jnp.dot(
            cells_out.at(u)[:, span], coders.at(u)[span, :], preferred_element_type=F32
        )

    def transport(i, u, between):
        source = cells_in.at(u)
        target = cells_out.at(u)
        for k in range(nb):
            block = blocks[i * nb + k]
            along, sign, weights = taps(block)
            parity = lax.rem(block, 2)
            level = consts[0] + along * consts[1] + (along * along) * consts[2]
            total = energy[...]
            for t in range(tiles):
                tile = k * tiles + t
                between(tile)
                lanes = slice(tile * LANES, (tile + 1) * LANES)
                far = pl.ds(pl.multiple_of(i * width + tile * LANES, LANES), LANES)
                fill(pad, tile, lanes, far, source, left, right, inflow, open_left, open_right)
                fstar = stencil(pad, tile, 8 - HALO, rows, sign, weights)
                full = fstar + (
                    SCALE * decoded[u % 2][0:rows, lanes] - (level + bands[parity, t])
                )
                ghost = inflow[:, far]
                state[tile, 0:8, :] = jnp.where(cut_top, ghost, full[0:8])
                state[tile, 8 : rows - 8, :] = full[8 : rows - 8]
                state[tile, rows - 8 : rows, :] = jnp.where(cut_bottom, ghost, full[rows - 8 :])
                again = stencil(state, tile, HALO, cells, sign, weights)
                y, z = pattern_rows(pats, parity, slice(t * LANES, (t + 1) * LANES))
                total = total + again * (along * along + (y * y + z * z))
                target[:, lanes] = again.astype(BF16)
            energy[...] = total

    def step(i, u, before=True, after=True):
        cells_in.wait(i, u)
        if after:
            coders.wait(i + 1, u + 1)
        if before:
            coders.start(i + RING - 2, u + RING - 2)
        cells_in.start(i + RING - 1, u + RING - 1)
        cells_out.drain(i, u)

        def between(tile):
            if before and tile % GROUP == 0:
                encode_part(u + RING - 1, tile, GROUP)
            if after and tile % GROUP == 0:
                decode_part(u + 1, tile, GROUP)

        transport(i, u, between)
        cells_out.start(i, u)

    coders.wait(0, 0)
    decode_part(0, 0, nb * tiles)
    step(0, 0, before=False)
    unrolled(1, steps - 1, step)
    last = steps - 1
    step(last, last, after=False)
    encode_part(last, 0, nb * tiles)
    message[0:cells, :] = sums[...].astype(BF16)
    put_parts(message, lambda k, r: cells, energy_row(energy[...], cells), 3, LANES)
    for i in range(max(0, steps - cells_out.slots), steps):
        cells_out.wait(i, i)


def third_kernel(
    nb, peers, blocks, source, coder, w_latent, b_latent, moments, restitution, *refs
):
    parts, refs = refs[:peers], refs[peers:]
    (
        out, decoded_a, decoded_b, result, pats, total, active, consts, bands,
        weights_in, sem_w, tiles_c, sem_c, tiles_d, sem_d, sem_o,
    ) = refs
    cells = source.shape[0]
    width = nb * WIDTH
    tiles = WIDTH // LANES
    load = pltpu.make_async_copy(w_latent, weights_in, sem_w)
    load.start()
    coders = Stream(coder, tiles_c, sem_c, width, 0)
    cells_in = Stream(source, tiles_d, sem_d, width, 1)
    cells_out = Stream(out, result, sem_o, width, 1, inward=False)
    coders.begin(RING)
    cells_in.begin(RING - 1)
    steps = coders.count
    decoded = (decoded_a, decoded_b)

    collect(parts[0], parts[1:], total)
    moment_pattern(pats)
    load.wait()
    latent_layer(total, weights_in, b_latent, active)
    project(
        active[0:cells, :].astype(F32), moments, energy_of(total, cells),
        diagonal(restitution[...], 0, cells), pats, consts, bands,
    )

    def decode_part(u, tile, count):
        span = slice(tile * LANES, (tile + count) * LANES)
        decoded[u % 2][:, span] = lax.dot_general(
            active[0:cells, :], coders.at(u)[span, :], (((1,), (1,)), ((), ())),
            preferred_element_type=F32,
        )

    def finish(i, u, between):
        here = cells_in.at(u)
        target = cells_out.at(u)
        for k in range(nb):
            block = blocks[i * nb + k]
            along = (2 * (block * WIDTH // (VGRID * VGRID)) + 1 - VGRID).astype(F32)
            parity = lax.rem(block, 2)
            level = consts[0] + along * consts[1] + (along * along) * consts[2]
            for t in range(tiles):
                tile = k * tiles + t
                between(tile)
                lanes = slice(tile * LANES, (tile + 1) * LANES)
                full = here[:, lanes].astype(F32) + (
                    SCALE * decoded[u % 2][:, lanes] - (level + bands[parity, t])
                )
                target[:, lanes] = full.astype(BF16)

    def step(i, u, after=True):
        cells_in.wait(i, u)
        if after:
            coders.wait(i + 1, u + 1)
        coders.start(i + RING, u)
        cells_in.start(i + RING - 1, u + RING - 1)
        cells_out.drain(i, u)

        def between(tile):
            if after and tile % GROUP == 0:
                decode_part(u + 1, tile, GROUP)

        finish(i, u, between)
        cells_out.start(i, u)

    coders.wait(0, 0)
    decode_part(0, 0, nb * tiles)
    unrolled(0, steps - 1, step)
    step(steps - 1, steps - 1, after=False)
    for i in range(max(0, steps - cells_out.slots), steps):
        cells_out.wait(i, i)


def shifted(array, axes, count, shift):
    return lax.ppermute(array, axes, [(i, (i + shift) % count) for i in range(count)])


def pieces(values):
    first = lax.reduce_precision(values, 8, 7)
    second = lax.reduce_precision(values - first, 8, 7)
    third = values - first - second
    return jnp.stack([first, second, third], -1).astype(BF16)


def spread(message):
    count = lax.axis_size("vel")
    return [message] + [shifted(message, "vel", count, s) for s in range(1, count)]


def body(density, coder, w_latent, b_latent, restitution, inflow, flags, blocks):
    cells, vels = density.shape
    count = blocks.shape[0]
    nb = 2 if count % 2 == 0 else 1
    width = nb * WIDTH
    tiles = width // LANES
    rows = cells + 2 * HALO
    ring = ("cell", "sub")
    ring_count = lax.axis_size("cell") * lax.axis_size("sub")
    peers = lax.axis_size("vel")

    def edge(part, r):
        extra = jnp.pad(pieces(r), ((0, 0), (0, LANES - 3)))
        return jnp.concatenate([part, extra], 1)

    left = shifted(edge(density[cells - HALO :], restitution[cells - HALO :]), ring, ring_count, 1)
    right = shifted(edge(density[:HALO], restitution[:HALO]), ring, ring_count, -1)
    inflow = inflow[None, :]
    restitution = restitution[None, :]
    b_latent = b_latent[None, :]

    shape = jax.ShapeDtypeStruct
    vmem = pl.BlockSpec(memory_space=pltpu.VMEM)
    smem = pl.BlockSpec(memory_space=pltpu.SMEM)
    hbm = pl.BlockSpec(memory_space=pl.ANY)
    params = pltpu.CompilerParams(vmem_limit_bytes=VMEM_MIB * 1024 * 1024)
    dma = pltpu.SemaphoreType.DMA
    coder_ring = [pltpu.VMEM((RING, width, LATENT), BF16), dma((RING,))]
    cells_ring = [pltpu.VMEM((RING, cells, width), BF16), dma((RING,))]
    latent_in = [pltpu.VMEM((LATENT, LATENT), BF16), dma(())]

    message = pl.pallas_call(
        functools.partial(first_kernel, nb),
        out_shape=shape((rows + 8, LATENT), BF16),
        in_specs=[smem, smem, hbm, vmem, vmem, vmem, hbm],
        out_specs=vmem,
        scratch_shapes=[
            pltpu.VMEM((tiles, rows + 8, LANES), F32),
            pltpu.VMEM((rows + 8, width), BF16),
            pltpu.VMEM((rows + 8, width), BF16),
            pltpu.VMEM((rows, LANES), F32),
            pltpu.VMEM((8, WIDTH), F32),
            pltpu.VMEM((rows + 8, LATENT), F32),
            *coder_ring,
            *cells_ring,
        ],
        compiler_params=params,
        name="first",
    )(blocks, flags, density, left, right, inflow, coder)

    coarse, message, moments = pl.pallas_call(
        functools.partial(second_kernel, nb, peers),
        out_shape=(
            shape((cells, vels), BF16), shape((cells + 8, LATENT), BF16), shape((8, LATENT), F32),
        ),
        in_specs=[smem, smem, hbm, vmem, vmem, vmem, hbm, hbm, vmem, vmem] + [vmem] * peers,
        out_specs=(hbm, vmem, vmem),
        scratch_shapes=[
            pltpu.VMEM((tiles, rows + 8, LANES), F32),
            pltpu.VMEM((tiles, rows, LANES), F32),
            pltpu.VMEM((rows + 8, width), F32),
            pltpu.VMEM((rows + 8, width), F32),
            pltpu.VMEM((2, cells, width), BF16),
            pltpu.VMEM((cells, LANES), F32),
            pltpu.VMEM((8, WIDTH), F32),
            pltpu.VMEM((cells, LATENT), F32),
            pltpu.VMEM((rows + 8, LATENT), F32),
            pltpu.VMEM((rows + 8, LATENT), BF16),
            pltpu.VMEM((3, rows, LANES), F32),
            pltpu.VMEM((2, WIDTH // LANES, rows, LANES), F32),
            *latent_in,
            *coder_ring,
            *cells_ring,
            dma((2,)),
        ],
        compiler_params=params,
        name="second",
    )(
        blocks, flags, density, left, right, inflow, coder, w_latent, b_latent, restitution,
        *spread(message),
    )

    return pl.pallas_call(
        functools.partial(third_kernel, nb, peers),
        out_shape=shape((cells, vels), BF16),
        in_specs=[smem, hbm, hbm, hbm, vmem, vmem, vmem] + [vmem] * peers,
        out_specs=hbm,
        scratch_shapes=[
            pltpu.VMEM((cells, width), F32),
            pltpu.VMEM((cells, width), F32),
            pltpu.VMEM((2, cells, width), BF16),
            pltpu.VMEM((8, WIDTH), F32),
            pltpu.VMEM((cells + 8, LATENT), F32),
            pltpu.VMEM((cells + 8, LATENT), BF16),
            pltpu.VMEM((3, cells, LANES), F32),
            pltpu.VMEM((2, WIDTH // LANES, cells, LANES), F32),
            *latent_in,
            *coder_ring,
            *cells_ring,
            dma((2,)),
        ],
        compiler_params=params,
        name="third",
    )(blocks, coarse, coder, w_latent, b_latent, moments, restitution, *spread(message))


def solution(mesh):
    return jax.shard_map(
        body,
        mesh=mesh,
        in_specs=(
            P(("groups", "cell", "sub"), "vel"),
            P("vel", None),
            P(),
            P(),
            P(("groups", "cell", "sub")),
            P(("groups", "vel")),
            P("groups"),
            P(("groups", "vel")),
        ),
        out_specs=P(("groups", "cell", "sub"), "vel"),
        check_vma=False,
    )
```

```python
import functools
import math

import jax
import jax.numpy as jnp
import numpy as np
from jax import lax
from jax.experimental import pallas as pl
from jax.experimental.pallas import tpu as pltpu
from jax.sharding import PartitionSpec as P

VGRID = 48
LATENT = 512
VBLOCKS = 96
STEPS = 2
VELS = 110592
WIDTH = VELS // VBLOCKS
LANES = 128
HALO = 4
SLOTS = 2
VMEM_MIB = 50
SINK_RATE = 0.5
COURANT = 0.9
SCALE = math.sqrt(VELS / LATENT)
F32 = jnp.float32
BF16 = jnp.bfloat16


def grid_moments():
    centres = (2.0 * np.arange(VGRID) + 1.0 - VGRID) / VGRID
    second = float(np.sum(centres**2))
    fourth = float(np.sum(centres**4))
    number = float(VGRID)
    total = number**3
    cross = 3.0 * number * number * second
    quartic = 3.0 * number * number * fourth + 6.0 * number * second * second
    square = number * number * second
    return (total, cross, quartic, square)


def moment_pattern(pats):
    number = lax.broadcasted_iota(jnp.int32, (1, WIDTH), 1).astype(F32)
    along_y = jnp.floor((number + 0.5) * (1.0 / VGRID))
    along_z = number - VGRID * along_y
    first = 2.0 * along_y + (1 - VGRID)
    pats[0:1, :] = first
    pats[1:2, :] = first + (2 * WIDTH // VGRID)
    pats[2:3, :] = 2.0 * along_z + (1 - VGRID)


def taps(block):
    along = 2 * (block * WIDTH // (VGRID * VGRID)) + 1 - VGRID
    sign = jnp.where(along >= 0, 1, -1)
    along = along.astype(F32)
    a = jnp.abs(along) * (COURANT / VGRID)
    upwind = (1.0 - a) * 0.5
    curved = (1.0 - a * a) * (1.0 / 6.0)
    far = -a * curved
    behind = a * (1.0 - upwind + 3.0 * curved)
    here = 1.0 - a * (1.0 - 2.0 * upwind + 3.0 * curved)
    ahead = -a * (upwind - curved)
    return along, sign, (far, behind, here, ahead)


def stencil(ref, tile, first, count, sign, weights):
    far, behind, here, ahead = weights
    at = lambda shift: ref[tile, pl.ds(first + shift, count), :]
    return (
        far * at(-2 * sign) + behind * at(-sign) + here * at(0) + ahead * at(sign)
    )


def fill(pad, tile, lanes, far_lanes, density, left, right, inflow, open_left, open_right):
    cells = density.shape[0]
    ghost = inflow[:, far_lanes]
    pad[tile, 8 : 8 + cells, :] = density[:, lanes].astype(F32)
    pad[tile, 8 - HALO : 8, :] = jnp.where(open_left, left[:, far_lanes].astype(F32), ghost)
    pad[tile, 8 + cells : 8 + cells + HALO, :] = jnp.where(
        open_right, right[:, far_lanes].astype(F32), ghost
    )


def energy_row(total, rows):
    column = jnp.sum(total, axis=1, keepdims=True) * (1.0 / (VGRID * VGRID))
    row = lax.broadcasted_iota(jnp.int32, (rows, LANES), 0)
    lane = lax.broadcasted_iota(jnp.int32, (rows, LANES), 1)
    return jnp.sum(jnp.where(row == lane, column, 0.0), axis=0, keepdims=True)


def pattern_rows(pats, parity, lanes):
    y = jnp.where(parity == 0, pats[0:1, lanes], pats[1:2, lanes])
    return y, pats[2:3, lanes]


def sides(flags):
    sub_count = lax.axis_size("sub")
    count = lax.axis_size("cell") * sub_count
    position = lax.axis_index("cell") * sub_count + lax.axis_index("sub")
    return flags[position] == 1, flags[lax.rem(position + 1, count)] == 1


class Stream:
    def __init__(self, source, buffers, sems, tile, axis, inward=True):
        self.source, self.buffers, self.sems = source, buffers, sems
        self.tile, self.axis, self.inward = tile, axis, inward
        self.count = source.shape[axis] // tile
        self.slots = buffers.shape[0]

    def copy(self, i, u):
        slot = u % self.slots
        span = pl.ds(pl.multiple_of(i * self.tile, LANES), self.tile)
        far = self.source.at[span, :] if self.axis == 0 else self.source.at[:, span]
        near = self.buffers.at[slot]
        source, target = (far, near) if self.inward else (near, far)
        return pltpu.make_async_copy(source, target, self.sems.at[slot])

    def begin(self, ahead):
        for i in range(min(ahead, self.count)):
            self.copy(i, i).start()

    def start(self, i, u):
        if isinstance(i, int):
            if i < self.count:
                self.copy(i, u).start()
        else:

            @pl.when(i < self.count)
            def _():
                self.copy(i, u).start()

    def wait(self, i, u):
        self.copy(i, u).wait()

    def drain(self, i, u):
        if isinstance(i, int):
            if i >= self.slots:
                self.wait(i - self.slots, u)
        else:

            @pl.when(i >= self.slots)
            def _():
                self.wait(i - self.slots, u)

    def at(self, u):
        return self.buffers.at[u % self.slots]


def unrolled(last, ring, step):
    first, trips = 0, last // ring
    if trips > 1:

        def trip(j, carry):
            for k in range(ring):
                step(ring * j + k, k)
            return carry

        lax.fori_loop(0, trips, trip, 0)
        first = ring * trips
    for i in range(first, last):
        step(i, i % ring)


def loads(pairs, sems):
    copies = [pltpu.make_async_copy(a, b, sems.at[k]) for k, (a, b) in enumerate(pairs)]
    for copy in copies:
        copy.start()

    def wait():
        for copy in copies:
            copy.wait()

    return wait


def put_parts(message, row_of, values, count, lane_step=0):
    height, width = values.shape
    for k in range(count):
        part = values.astype(BF16)
        values = values - part.astype(F32)
        for r in range(height):
            lanes = slice(k * lane_step, k * lane_step + width)
            message[row_of(k, r) : row_of(k, r) + 1, lanes] = part[r : r + 1]


def moment_row(rows, k, r):
    place = 5 * k + r
    return rows + place if place < 8 else rows - 2 + (place - 8)


def first_kernel(
    nb, blocks_in, flags_in, density, left_in, right_in, inflow_in, coder, message, *refs
):
    (
        pad, coarse_a, coarse_b, energy, pats, sums, blocks, flags, left, right, inflow, sem_s,
        tiles_c, sem_c, tiles_d, sem_d,
    ) = refs
    cells = density.shape[0]
    rows = cells + 2 * HALO
    width = nb * WIDTH
    tiles = WIDTH // LANES
    coders = Stream(coder, tiles_c, sem_c, width, 0)
    cells_in = Stream(density, tiles_d, sem_d, width, 1)
    cells_in.begin(1)
    wait = loads(
        (
            (left_in, left), (right_in, right), (inflow_in, inflow),
            (blocks_in, blocks), (flags_in, flags),
        ),
        sem_s,
    )
    ahead = coders.slots - 1
    coders.begin(ahead)
    for i in range(1, min(ahead, cells_in.count)):
        cells_in.copy(i, i).start()
    steps = coders.count
    coarse = (coarse_a, coarse_b)

    moment_pattern(pats)
    sums[...] = jnp.zeros_like(sums)
    energy[...] = jnp.zeros_like(energy)
    pad[...] = jnp.zeros_like(pad)
    wait()
    open_left, open_right = sides(flags)
    kind = lax.broadcasted_iota(jnp.int32, (8, LANES), 0)

    def transport(i, u):
        source = cells_in.at(u)
        for k in range(nb):
            block = blocks[i * nb + k]
            along, sign, weights = taps(block)
            parity = lax.rem(block, 2)
            total = energy[...]
            for t in range(tiles):
                tile = k * tiles + t
                lanes = slice(tile * LANES, (tile + 1) * LANES)
                far = pl.ds(pl.multiple_of(i * width + tile * LANES, LANES), LANES)
                fill(pad, tile, lanes, far, source, left, right, inflow, open_left, open_right)
                fstar = stencil(pad, tile, 8 - HALO, rows, sign, weights)
                y, z = pattern_rows(pats, parity, slice(t * LANES, (t + 1) * LANES))
                e = along * along + (y * y + z * z)
                total = total + fstar * e
                high = e.astype(BF16).astype(F32)
                basis = jnp.where(kind == 0, 1.0, 0.0)
                basis = jnp.where(kind == 1, along, basis)
                basis = jnp.where(kind == 2, y, basis)
                basis = jnp.where(kind == 3, z, basis)
                basis = jnp.where(kind == 4, high, basis)
                basis = jnp.where(kind == 5, e - high, basis)
                coarse[u % 2][:, lanes] = jnp.concatenate([fstar, basis], 0).astype(BF16)
            energy[...] = total

    def encode(u):
        sums[...] += jnp.dot(coarse[u % 2][...], coders.at(u)[...], preferred_element_type=F32)

    def step(i, u):
        cells_in.wait(i, u)
        coders.wait(i, u)
        coders.start(i + ahead, u + ahead)
        cells_in.start(i + ahead, u + ahead)
        transport(i, u)
        encode(u)

    unrolled(steps, coders.slots, step)

    base = sums[rows : rows + 1, :]
    base = base.astype(BF16).astype(F32) + (base - base.astype(BF16).astype(F32)).astype(BF16)
    message[0:rows, :] = (sums[0:rows, :] - base).astype(BF16)
    last = sums[rows + 4 : rows + 5, :] + sums[rows + 5 : rows + 6, :]
    moments = jnp.concatenate([sums[rows : rows + 4, :], last], 0)
    put_parts(message, functools.partial(moment_row, rows), moments, 2)
    put_parts(message, lambda k, r: 0, energy_row(energy[...], rows), 3, LANES)


def project(act, moments, energy, restitution, pats, consts, bands):
    total, cross, quartic, square = grid_moments()
    determinant = total * quartic - cross * cross
    rows = restitution.shape[0]
    inverse = 1.0 / VGRID
    dots = [
        SCALE * jnp.sum(act * moments[k : k + 1, :], axis=1, keepdims=True) for k in range(5)
    ]
    row = lax.broadcasted_iota(jnp.int32, (rows, LANES), 0)
    lane = lax.broadcasted_iota(jnp.int32, (rows, LANES), 1)
    energy_sum = jnp.sum(jnp.where(row == lane, energy, 0.0), axis=1, keepdims=True)
    sink = -SINK_RATE * (1.0 - restitution * restitution) * energy_sum
    excess = dots[4] * (inverse * inverse) - sink
    mass = (quartic * dots[0] - cross * excess) / determinant
    power = (total * excess - cross * dots[0]) / determinant * (inverse * inverse)
    slopes = [dots[k] * (inverse * inverse / square) for k in (1, 2, 3)]
    spread = lambda column: jnp.broadcast_to(column, (rows, LANES))
    consts[0] = spread(mass)
    consts[1] = spread(slopes[0])
    consts[2] = spread(power)
    power, second, third = spread(power), spread(slopes[1]), spread(slopes[2])
    for parity in range(2):
        for t in range(WIDTH // LANES):
            lanes = slice(t * LANES, (t + 1) * LANES)
            y, z = pats[parity : parity + 1, lanes], pats[2:3, lanes]
            bands[parity, t] = second * y + third * z + power * (y * y + z * z)


def diagonal(row, first, rows):
    shape = (rows, row.shape[1])
    place = lax.broadcasted_iota(jnp.int32, shape, 0) - first
    lane = lax.broadcasted_iota(jnp.int32, shape, 1)
    return jnp.sum(jnp.where(place == lane, row, 0.0), axis=1, keepdims=True)


def collect(parts, total):
    total[...] = sum(parts[k].astype(F32) for k in range(parts.shape[0]))


def energy_of(total, row):
    return sum(total[row : row + 1, k * LANES : (k + 1) * LANES] for k in range(3))


def latent_layer(total, w_latent, b_latent, active):
    mixed = jnp.dot(total[...].astype(BF16), w_latent[...], preferred_element_type=F32)
    active[...] = jnp.tanh(mixed + b_latent[...]).astype(BF16)


def diagonal(row, first, rows):
    shape = (rows, row.shape[1])
    place = lax.broadcasted_iota(jnp.int32, shape, 0) - first
    lane = lax.broadcasted_iota(jnp.int32, shape, 1)
    return jnp.sum(jnp.where(place == lane, row, 0.0), axis=1, keepdims=True)


def second_kernel(
    nb, peers, blocks_in, flags_in, density, left_in, right_in, inflow_in, coder, w_latent,
    b_latent, restitution, *refs
):
    parts_in, refs = refs[:peers], refs[peers:]
    (
        out, message, moments, pad, state, coarse, energy, pats, sums,
        total, active, consts, bands, weights, parts, blocks, flags, left, right, inflow, sem_s,
        tiles_c, sem_c, tiles_d, sem_d, sem_o, *decoded,
    ) = refs
    cells = density.shape[0]
    rows = cells + 2 * HALO
    width = nb * WIDTH
    tiles = WIDTH // LANES
    wait = loads(
        [(part, parts.at[k]) for k, part in enumerate(parts_in)]
        + [(w_latent, weights), (left_in, left), (right_in, right), (inflow_in, inflow)]
        + [(blocks_in, blocks), (flags_in, flags)],
        sem_s,
    )
    coders = Stream(coder, tiles_c, sem_c, width, 0)
    cells_in = Stream(density, tiles_d, sem_d, width, 1)
    cells_out = Stream(out, coarse, sem_o, width, 1, inward=False)
    ahead = coders.slots - 1
    coders.begin(ahead)
    cells_in.begin(ahead)
    steps = coders.count
    group = 3 if nb * tiles % 2 else 2
    vels = density.shape[1]

    moment_pattern(pats)
    sums[...] = jnp.zeros_like(sums)
    energy[...] = jnp.zeros_like(energy)
    pad[...] = jnp.zeros_like(pad)
    wait()
    open_left, open_right = sides(flags)
    collect(parts, total)
    for r in range(5):
        at = [moment_row(rows, k, r) for k in range(2)]
        moments[r : r + 1, :] = total[at[0] : at[0] + 1, :] + total[at[1] : at[1] + 1, :]
    ghosts = [jnp.sum(side[:, vels:].astype(F32), axis=1, keepdims=True) for side in (left, right)]
    r = diagonal(restitution[...], HALO, rows)
    state[0, 0:rows, :] = jnp.broadcast_to(r, (rows, LANES))
    state[0, 0:HALO, :] = jnp.broadcast_to(ghosts[0], (HALO, LANES))
    state[0, HALO + cells : rows, :] = jnp.broadcast_to(ghosts[1], (HALO, LANES))
    energy_row_in = energy_of(total, 0)
    base = sum(
        parts[0, at : at + 1, :].astype(F32) for at in (rows, moment_row(rows, 1, 0))
    )
    total[...] += moments[0:1, :]
    latent_layer(total, weights, b_latent, active)
    project(
        active[0:rows, :].astype(F32), moments, energy_row_in, state[0, :, 0:1],
        pats, consts, bands,
    )
    place = lax.broadcasted_iota(jnp.int32, (8, LANES), 0)
    cut_top = jnp.logical_and(place < HALO, jnp.logical_not(open_left))
    cut_bottom = jnp.logical_and(place >= 8 - HALO, jnp.logical_not(open_right))

    def decode_part(u, tile):
        span = slice(tile * LANES, (tile + group) * LANES)
        decoded[tile // group % SLOTS][...] = lax.dot_general(
            active[...], coders.at(u)[span, :], (((1,), (1,)), ((), ())),
            preferred_element_type=F32,
        )

    def encode(u):
        sums[...] += jnp.dot(
            cells_out.at(u)[...], coders.at(u)[...], preferred_element_type=F32
        )

    def transport(i, u):
        source = cells_in.at(u)
        target = cells_out.at(u)
        for k in range(nb):
            block = blocks[i * nb + k]
            along, sign, weights = taps(block)
            parity = lax.rem(block, 2)
            level = consts[0] + along * consts[1] + (along * along) * consts[2]
            total = energy[...]
            for t in range(tiles):
                tile = k * tiles + t
                if tile % group == 0:
                    decode_part(u, tile)
                lanes = slice(tile * LANES, (tile + 1) * LANES)
                far = pl.ds(pl.multiple_of(i * width + tile * LANES, LANES), LANES)
                fill(pad, tile, lanes, far, source, left, right, inflow, open_left, open_right)
                fstar = stencil(pad, tile, 8 - HALO, rows, sign, weights)
                full = fstar + (
                    SCALE * decoded[tile // group % SLOTS][0:rows, slice(tile % group * LANES, (tile % group + 1) * LANES)]
                    - (level + bands[parity, t])
                )
                ghost = inflow[:, far]
                state[tile, 0:8, :] = jnp.where(cut_top, ghost, full[0:8])
                state[tile, 8 : rows - 8, :] = full[8 : rows - 8]
                state[tile, rows - 8 : rows, :] = jnp.where(cut_bottom, ghost, full[rows - 8 :])
                again = stencil(state, tile, HALO, cells, sign, weights)
                y, z = pattern_rows(pats, parity, slice(t * LANES, (t + 1) * LANES))
                total = total + again * (along * along + (y * y + z * z))
                target[:, lanes] = again.astype(BF16)
            energy[...] = total

    def step(i, u):
        cells_in.wait(i, u)
        coders.wait(i, u)
        coders.start(i + ahead, u + ahead)
        cells_in.start(i + ahead, u + ahead)
        cells_out.drain(i, u)
        transport(i, u)
        encode(u)
        cells_out.start(i, u)

    unrolled(steps, coders.slots, step)
    message[0:cells, :] = (sums[...] - base).astype(BF16)
    put_parts(message, lambda k, r: cells, energy_row(energy[...], cells), 3, LANES)
    for i in range(max(0, steps - cells_out.slots), steps):
        cells_out.wait(i, i)


def third_kernel(
    nb, peers, blocks_in, source, coder, w_latent, b_latent, moments, restitution, *refs
):
    parts_in, refs = refs[:peers], refs[peers:]
    (
        out, result, pats, total, active, consts, bands,
        weights, parts, blocks, sem_s, tiles_c, sem_c, tiles_d, sem_d, sem_o, *decoded,
    ) = refs
    cells = source.shape[0]
    width = nb * WIDTH
    tiles = WIDTH // LANES
    wait = loads(
        [(part, parts.at[k]) for k, part in enumerate(parts_in)]
        + [(w_latent, weights), (blocks_in, blocks)],
        sem_s,
    )
    coders = Stream(coder, tiles_c, sem_c, width, 0)
    cells_in = Stream(source, tiles_d, sem_d, width, 1)
    cells_out = Stream(out, result, sem_o, width, 1, inward=False)
    ahead = coders.slots - 1
    coders.begin(ahead)
    cells_in.begin(ahead)
    steps = coders.count
    group = 3 if nb * tiles % 2 else 2

    moment_pattern(pats)
    wait()
    collect(parts, total)
    energy_row_in = energy_of(total, cells)
    total[...] += moments[0:1, :]
    latent_layer(total, weights, b_latent, active)
    project(
        active[0:cells, :].astype(F32), moments, energy_row_in,
        diagonal(restitution[...], 0, cells), pats, consts, bands,
    )

    def decode_part(u, tile):
        span = slice(tile * LANES, (tile + group) * LANES)
        decoded[tile // group % SLOTS][...] = lax.dot_general(
            active[0:cells, :], coders.at(u)[span, :], (((1,), (1,)), ((), ())),
            preferred_element_type=F32,
        )

    def finish(i, u):
        here = cells_in.at(u)
        target = cells_out.at(u)
        for k in range(nb):
            block = blocks[i * nb + k]
            along = (2 * (block * WIDTH // (VGRID * VGRID)) + 1 - VGRID).astype(F32)
            parity = lax.rem(block, 2)
            level = consts[0] + along * consts[1] + (along * along) * consts[2]
            for t in range(tiles):
                tile = k * tiles + t
                if tile % group == 0:
                    decode_part(u, tile)
                lanes = slice(tile * LANES, (tile + 1) * LANES)
                full = here[:, lanes].astype(F32) + (
                    SCALE * decoded[tile // group % SLOTS][:, slice(tile % group * LANES, (tile % group + 1) * LANES)]
                    - (level + bands[parity, t])
                )
                target[:, lanes] = full.astype(BF16)

    def step(i, u):
        cells_in.wait(i, u)
        coders.wait(i, u)
        coders.start(i + ahead, u + ahead)
        cells_in.start(i + ahead, u + ahead)
        cells_out.drain(i, u)
        finish(i, u)
        cells_out.start(i, u)

    unrolled(steps, coders.slots, step)
    for i in range(max(0, steps - cells_out.slots), steps):
        cells_out.wait(i, i)


def shifted(array, axes, count, shift):
    return lax.ppermute(array, axes, [(i, (i + shift) % count) for i in range(count)])


def pieces(values):
    first = lax.reduce_precision(values, 8, 7)
    second = lax.reduce_precision(values - first, 8, 7)
    third = values - first - second
    return jnp.stack([first, second, third], -1).astype(BF16)


def spread(message):
    count = lax.axis_size("vel")
    return [message] + [shifted(message, "vel", count, s) for s in range(1, count)]


def body(density, coder, w_latent, b_latent, restitution, inflow, flags, blocks):
    cells, vels = density.shape
    count = blocks.shape[0]
    tiles = WIDTH // LANES
    rows = cells + 2 * HALO
    ring = ("cell", "sub")
    ring_count = lax.axis_size("cell") * lax.axis_size("sub")
    peers = lax.axis_size("vel")

    def edge(part, r):
        extra = jnp.pad(pieces(r), ((0, 0), (0, LANES - 3)))
        return jnp.concatenate([part, extra], 1)

    left = shifted(edge(density[cells - HALO :], restitution[cells - HALO :]), ring, ring_count, 1)
    right = shifted(edge(density[:HALO], restitution[:HALO]), ring, ring_count, -1)
    inflow = inflow[None, :]
    restitution = restitution[None, :]
    b_latent = b_latent[None, :]

    shape = jax.ShapeDtypeStruct
    vmem = pl.BlockSpec(memory_space=pltpu.VMEM)
    hbm = pl.BlockSpec(memory_space=pltpu.HBM)
    free = pl.BlockSpec(memory_space=pl.ANY)
    counts = [pltpu.SMEM((count,), jnp.int32), pltpu.SMEM(flags.shape, jnp.int32)]
    limit = VMEM_MIB * 1024 * 1024
    params = pltpu.CompilerParams(vmem_limit_bytes=limit)
    spaced = pltpu.CompilerParams(
        vmem_limit_bytes=limit
    )
    dma = pltpu.SemaphoreType.DMA

    def rings(nb, slots):
        width = nb * WIDTH
        return [
            pltpu.VMEM((slots, width, LATENT), BF16), dma((slots,)),
            pltpu.VMEM((slots, cells, width), BF16), dma((slots,)),
        ]

    def tiling(*choices):
        return next((nb, slots) for nb, slots in choices + ((1, 3),) if count % nb == 0)

    edges = [pltpu.VMEM((HALO, vels + LANES), BF16)] * 2 + [pltpu.VMEM((1, vels), F32)]
    latent_in = pltpu.VMEM((LATENT, LATENT), BF16)
    nb, slots = tiling((2, 4))
    width = nb * WIDTH

    message = pl.pallas_call(
        functools.partial(first_kernel, nb),
        out_shape=shape((rows + 8, LATENT), BF16),
        in_specs=[hbm, hbm, hbm, free, free, hbm, hbm],
        out_specs=vmem,
        scratch_shapes=[
            pltpu.VMEM((nb * tiles, rows + 8, LANES), F32),
            pltpu.VMEM((rows + 8, width), BF16),
            pltpu.VMEM((rows + 8, width), BF16),
            pltpu.VMEM((rows, LANES), F32),
            pltpu.VMEM((8, WIDTH), F32),
            pltpu.VMEM((rows + 8, LATENT), F32),
            *counts,
            *edges,
            dma((5,)),
            *rings(nb, slots),
        ],
        compiler_params=spaced,
        name="first",
    )(blocks, flags, density, left, right, inflow, coder)

    nb, slots = tiling((4, 3), (2, 4))
    width = nb * WIDTH
    group = 3 if nb * tiles % 2 else 2
    coarse, message, moments = pl.pallas_call(
        functools.partial(second_kernel, nb, peers),
        out_shape=(
            shape((cells, vels), BF16), shape((cells + 8, LATENT), BF16), shape((8, LATENT), F32),
        ),
        in_specs=[hbm, hbm, hbm, free, free, hbm, hbm, free, vmem, vmem] + [free] * peers,
        out_specs=(hbm, vmem, vmem),
        scratch_shapes=[
            pltpu.VMEM((nb * tiles, rows + 8, LANES), F32),
            pltpu.VMEM((nb * tiles, rows, LANES), F32),
            pltpu.VMEM((2, cells, width), BF16),
            pltpu.VMEM((cells, LANES), F32),
            pltpu.VMEM((8, WIDTH), F32),
            pltpu.VMEM((cells, LATENT), F32),
            pltpu.VMEM((rows + 8, LATENT), F32),
            pltpu.VMEM((rows + 8, LATENT), BF16),
            pltpu.VMEM((3, rows, LANES), F32),
            pltpu.VMEM((2, WIDTH // LANES, rows, LANES), F32),
            latent_in,
            pltpu.VMEM((peers, rows + 8, LATENT), BF16),
            *counts,
            *edges,
            dma((peers + 6,)),
            *rings(nb, slots),
            dma((2,)),
            *[pltpu.VMEM((rows + 8, group * LANES), F32)] * SLOTS,
        ],
        compiler_params=params,
        name="second",
    )(
        blocks, flags, density, left, right, inflow, coder, w_latent, b_latent, restitution,
        *spread(message),
    )

    nb, slots = tiling((2, 4))
    width = nb * WIDTH
    group = 3 if nb * tiles % 2 else 2
    return pl.pallas_call(
        functools.partial(third_kernel, nb, peers),
        out_shape=shape((cells, vels), BF16),
        in_specs=[hbm, hbm, hbm, free, vmem, vmem, vmem] + [free] * peers,
        out_specs=hbm,
        scratch_shapes=[
            pltpu.VMEM((2, cells, width), BF16),
            pltpu.VMEM((8, WIDTH), F32),
            pltpu.VMEM((cells + 8, LATENT), F32),
            pltpu.VMEM((cells + 8, LATENT), BF16),
            pltpu.VMEM((3, cells, LANES), F32),
            pltpu.VMEM((2, WIDTH // LANES, cells, LANES), F32),
            latent_in,
            pltpu.VMEM((peers, cells + 8, LATENT), BF16),
            counts[0],
            dma((peers + 2,)),
            *rings(nb, slots),
            dma((2,)),
            *[pltpu.VMEM((cells, group * LANES), F32)] * SLOTS,
        ],
        compiler_params=params,
        name="third",
    )(blocks, coarse, coder, w_latent, b_latent, moments, restitution, *spread(message))


def solution(mesh):
    return jax.shard_map(
        body,
        mesh=mesh,
        in_specs=(
            P(("groups", "cell", "sub"), "vel"),
            P("vel", None),
            P(),
            P(),
            P(("groups", "cell", "sub")),
            P(("groups", "vel")),
            P("groups"),
            P(("groups", "vel")),
        ),
        out_specs=P(("groups", "cell", "sub"), "vel"),
        check_vma=False,
    )
```

```python
import functools
import math

import jax
import jax.numpy as jnp
import numpy as np
from jax import lax
from jax.experimental import pallas as pl
from jax.experimental.pallas import tpu as pltpu
from jax.sharding import PartitionSpec as P

VGRID = 48
LATENT = 512
VBLOCKS = 96
STEPS = 2
VELS = 110592
WIDTH = VELS // VBLOCKS
LANES = 128
HALO = 4
SLOTS = 2
VMEM_MIB = 50
SINK_RATE = 0.5
COURANT = 0.9
SCALE = math.sqrt(VELS / LATENT)
F32 = jnp.float32
BF16 = jnp.bfloat16


def grid_moments():
    centres = (2.0 * np.arange(VGRID) + 1.0 - VGRID) / VGRID
    second = float(np.sum(centres**2))
    fourth = float(np.sum(centres**4))
    number = float(VGRID)
    total = number**3
    cross = 3.0 * number * number * second
    quartic = 3.0 * number * number * fourth + 6.0 * number * second * second
    square = number * number * second
    return (total, cross, quartic, square)


def moment_pattern(pats):
    number = lax.broadcasted_iota(jnp.int32, (1, WIDTH), 1).astype(F32)
    along_y = jnp.floor((number + 0.5) * (1.0 / VGRID))
    along_z = number - VGRID * along_y
    first = 2.0 * along_y + (1 - VGRID)
    pats[0:1, :] = first
    pats[1:2, :] = first + (2 * WIDTH // VGRID)
    pats[2:3, :] = 2.0 * along_z + (1 - VGRID)


def taps(block):
    along = 2 * (block * WIDTH // (VGRID * VGRID)) + 1 - VGRID
    sign = jnp.where(along >= 0, 1, -1)
    along = along.astype(F32)
    a = jnp.abs(along) * (COURANT / VGRID)
    upwind = (1.0 - a) * 0.5
    curved = (1.0 - a * a) * (1.0 / 6.0)
    far = -a * curved
    behind = a * (1.0 - upwind + 3.0 * curved)
    here = 1.0 - a * (1.0 - 2.0 * upwind + 3.0 * curved)
    ahead = -a * (upwind - curved)
    return along, sign, (far, behind, here, ahead)


def stencil(ref, tile, first, count, sign, weights):
    far, behind, here, ahead = weights
    at = lambda shift: ref[tile, pl.ds(first + shift, count), :]
    return (
        far * at(-2 * sign) + behind * at(-sign) + here * at(0) + ahead * at(sign)
    )


def fill(pad, tile, lanes, far_lanes, density, left, right, inflow, open_left, open_right):
    cells = density.shape[0]
    ghost = inflow[:, far_lanes]
    pad[tile, 8 : 8 + cells, :] = density[:, lanes].astype(F32)
    pad[tile, 8 - HALO : 8, :] = jnp.where(open_left, left[:, far_lanes].astype(F32), ghost)
    pad[tile, 8 + cells : 8 + cells + HALO, :] = jnp.where(
        open_right, right[:, far_lanes].astype(F32), ghost
    )


def energy_row(total, rows):
    column = jnp.sum(total, axis=1, keepdims=True) * (1.0 / (VGRID * VGRID))
    row = lax.broadcasted_iota(jnp.int32, (rows, LANES), 0)
    lane = lax.broadcasted_iota(jnp.int32, (rows, LANES), 1)
    return jnp.sum(jnp.where(row == lane, column, 0.0), axis=0, keepdims=True)


def pattern_rows(pats, parity, lanes):
    y = jnp.where(parity == 0, pats[0:1, lanes], pats[1:2, lanes])
    return y, pats[2:3, lanes]


def sides(flags):
    sub_count = lax.axis_size("sub")
    count = lax.axis_size("cell") * sub_count
    position = lax.axis_index("cell") * sub_count + lax.axis_index("sub")
    return flags[position] == 1, flags[lax.rem(position + 1, count)] == 1


class Stream:
    def __init__(self, source, buffers, sems, tile, axis, inward=True):
        self.source, self.buffers, self.sems = source, buffers, sems
        self.tile, self.axis, self.inward = tile, axis, inward
        self.count = source.shape[axis] // tile
        self.slots = buffers.shape[0]

    def copy(self, i, u):
        slot = u % self.slots
        span = pl.ds(pl.multiple_of(i * self.tile, LANES), self.tile)
        far = self.source.at[span, :] if self.axis == 0 else self.source.at[:, span]
        near = self.buffers.at[slot]
        source, target = (far, near) if self.inward else (near, far)
        return pltpu.make_async_copy(source, target, self.sems.at[slot])

    def begin(self, ahead):
        for i in range(min(ahead, self.count)):
            self.copy(i, i).start()

    def start(self, i, u):
        if isinstance(i, int):
            if i < self.count:
                self.copy(i, u).start()
        else:

            @pl.when(i < self.count)
            def _():
                self.copy(i, u).start()

    def wait(self, i, u):
        self.copy(i, u).wait()

    def drain(self, i, u):
        if isinstance(i, int):
            if i >= self.slots:
                self.wait(i - self.slots, u)
        else:

            @pl.when(i >= self.slots)
            def _():
                self.wait(i - self.slots, u)

    def at(self, u):
        return self.buffers.at[u % self.slots]


def unrolled(last, ring, step):
    first, trips = 0, last // ring
    if trips > 1:

        def trip(j, carry):
            for k in range(ring):
                step(ring * j + k, k)
            return carry

        lax.fori_loop(0, trips, trip, 0)
        first = ring * trips
    for i in range(first, last):
        step(i, i % ring)


def loads(pairs, sems):
    copies = [pltpu.make_async_copy(a, b, sems.at[k]) for k, (a, b) in enumerate(pairs)]
    for copy in copies:
        copy.start()

    def wait():
        for copy in copies:
            copy.wait()

    return wait


def put_parts(message, row_of, values, count, lane_step=0):
    height, width = values.shape
    for k in range(count):
        part = values.astype(BF16)
        values = values - part.astype(F32)
        for r in range(height):
            lanes = slice(k * lane_step, k * lane_step + width)
            message[row_of(k, r) : row_of(k, r) + 1, lanes] = part[r : r + 1]


def moment_row(rows, k, r):
    place = 5 * k + r
    return rows + place if place < 8 else rows - 2 + (place - 8)


def first_kernel(
    nb, offset, numbers_in, density, left_in, right_in, inflow_in, coder, message, *refs
):
    (
        pad, coarse_a, coarse_b, energy, pats, sums, numbers, left, right, inflow, sem_s,
        tiles_c, sem_c, tiles_d, sem_d,
    ) = refs
    cells = density.shape[0]
    rows = cells + 2 * HALO
    width = nb * WIDTH
    tiles = WIDTH // LANES
    coders = Stream(coder, tiles_c, sem_c, width, 0)
    cells_in = Stream(density, tiles_d, sem_d, width, 1)
    cells_in.begin(1)
    wait = loads(
        (
            (left_in, left), (right_in, right), (inflow_in, inflow),
            (numbers_in, numbers),
        ),
        sem_s,
    )
    ahead = coders.slots - 1
    coders.begin(ahead)
    for i in range(1, min(ahead, cells_in.count)):
        cells_in.copy(i, i).start()
    steps = coders.count
    coarse = (coarse_a, coarse_b)

    moment_pattern(pats)
    sums[...] = jnp.zeros_like(sums)
    energy[...] = jnp.zeros_like(energy)
    pad[...] = jnp.zeros_like(pad)
    wait()
    open_left, open_right = sides(numbers)
    kind = lax.broadcasted_iota(jnp.int32, (8, LANES), 0)

    def transport(i, u):
        source = cells_in.at(u)
        for k in range(nb):
            block = numbers[offset + i * nb + k]
            along, sign, weights = taps(block)
            parity = lax.rem(block, 2)
            total = energy[...]
            for t in range(tiles):
                tile = k * tiles + t
                lanes = slice(tile * LANES, (tile + 1) * LANES)
                far = pl.ds(pl.multiple_of(i * width + tile * LANES, LANES), LANES)
                fill(pad, tile, lanes, far, source, left, right, inflow, open_left, open_right)
                fstar = stencil(pad, tile, 8 - HALO, rows, sign, weights)
                y, z = pattern_rows(pats, parity, slice(t * LANES, (t + 1) * LANES))
                e = along * along + (y * y + z * z)
                total = total + fstar * e
                high = e.astype(BF16).astype(F32)
                basis = jnp.where(kind == 0, 1.0, 0.0)
                basis = jnp.where(kind == 1, along, basis)
                basis = jnp.where(kind == 2, y, basis)
                basis = jnp.where(kind == 3, z, basis)
                basis = jnp.where(kind == 4, high, basis)
                basis = jnp.where(kind == 5, e - high, basis)
                coarse[u % 2][:, lanes] = jnp.concatenate([fstar, basis], 0).astype(BF16)
            energy[...] = total

    def encode(u):
        sums[...] += jnp.dot(coarse[u % 2][...], coders.at(u)[...], preferred_element_type=F32)

    def step(i, u):
        cells_in.wait(i, u)
        coders.wait(i, u)
        coders.start(i + ahead, u + ahead)
        cells_in.start(i + ahead, u + ahead)
        transport(i, u)
        encode(u)

    unrolled(steps, coders.slots, step)

    base = sums[rows : rows + 1, :]
    base = base.astype(BF16).astype(F32) + (base - base.astype(BF16).astype(F32)).astype(BF16)
    message[0:rows, :] = (sums[0:rows, :] - base).astype(BF16)
    last = sums[rows + 4 : rows + 5, :] + sums[rows + 5 : rows + 6, :]
    moments = jnp.concatenate([sums[rows : rows + 4, :], last], 0)
    put_parts(message, functools.partial(moment_row, rows), moments, 2)
    put_parts(message, lambda k, r: 0, energy_row(energy[...], rows), 3, LANES)


def project(act, moments, energy, restitution, pats, consts, bands):
    total, cross, quartic, square = grid_moments()
    determinant = total * quartic - cross * cross
    rows = restitution.shape[0]
    inverse = 1.0 / VGRID
    dots = [
        SCALE * jnp.sum(act * moments[k : k + 1, :], axis=1, keepdims=True) for k in range(5)
    ]
    row = lax.broadcasted_iota(jnp.int32, (rows, LANES), 0)
    lane = lax.broadcasted_iota(jnp.int32, (rows, LANES), 1)
    energy_sum = jnp.sum(jnp.where(row == lane, energy, 0.0), axis=1, keepdims=True)
    sink = -SINK_RATE * (1.0 - restitution * restitution) * energy_sum
    excess = dots[4] * (inverse * inverse) - sink
    mass = (quartic * dots[0] - cross * excess) / determinant
    power = (total * excess - cross * dots[0]) / determinant * (inverse * inverse)
    slopes = [dots[k] * (inverse * inverse / square) for k in (1, 2, 3)]
    spread = lambda column: jnp.broadcast_to(column, (rows, LANES))
    consts[0] = spread(mass)
    consts[1] = spread(slopes[0])
    consts[2] = spread(power)
    power, second, third = spread(power), spread(slopes[1]), spread(slopes[2])
    for parity in range(2):
        for t in range(WIDTH // LANES):
            lanes = slice(t * LANES, (t + 1) * LANES)
            y, z = pats[parity : parity + 1, lanes], pats[2:3, lanes]
            bands[parity, t] = second * y + third * z + power * (y * y + z * z)


def diagonal(row, first, rows):
    shape = (rows, row.shape[1])
    place = lax.broadcasted_iota(jnp.int32, shape, 0) - first
    lane = lax.broadcasted_iota(jnp.int32, shape, 1)
    return jnp.sum(jnp.where(place == lane, row, 0.0), axis=1, keepdims=True)


def collect(parts, total):
    total[...] = sum(parts[k].astype(F32) for k in range(parts.shape[0]))


def energy_of(total, row):
    return sum(total[row : row + 1, k * LANES : (k + 1) * LANES] for k in range(3))


def latent_layer(total, w_latent, b_latent, active):
    mixed = jnp.dot(total[...].astype(BF16), w_latent[...], preferred_element_type=F32)
    active[...] = jnp.tanh(mixed + b_latent[...]).astype(BF16)


def diagonal(row, first, rows):
    shape = (rows, row.shape[1])
    place = lax.broadcasted_iota(jnp.int32, shape, 0) - first
    lane = lax.broadcasted_iota(jnp.int32, shape, 1)
    return jnp.sum(jnp.where(place == lane, row, 0.0), axis=1, keepdims=True)


def second_kernel(
    nb, offset, peers, numbers_in, density, left_in, right_in, inflow_in, coder, w_latent,
    b_latent, restitution, *refs
):
    parts_in, refs = refs[:peers], refs[peers:]
    (
        out, message, moments, pad, state, coarse, energy, pats, sums,
        total, active, consts, bands, weights, parts, numbers, left, right, inflow, sem_s,
        tiles_c, sem_c, tiles_d, sem_d, sem_o, *decoded,
    ) = refs
    cells = density.shape[0]
    rows = cells + 2 * HALO
    width = nb * WIDTH
    tiles = WIDTH // LANES
    wait = loads(
        [(part, parts.at[k]) for k, part in enumerate(parts_in)]
        + [(w_latent, weights), (left_in, left), (right_in, right), (inflow_in, inflow)]
        + [(numbers_in, numbers)],
        sem_s,
    )
    coders = Stream(coder, tiles_c, sem_c, width, 0)
    cells_in = Stream(density, tiles_d, sem_d, width, 1)
    cells_out = Stream(out, coarse, sem_o, width, 1, inward=False)
    ahead = coders.slots - 1
    coders.begin(ahead)
    cells_in.begin(ahead)
    steps = coders.count
    group = 3 if nb * tiles % 2 else 2
    vels = density.shape[1]

    moment_pattern(pats)
    sums[...] = jnp.zeros_like(sums)
    energy[...] = jnp.zeros_like(energy)
    pad[...] = jnp.zeros_like(pad)
    wait()
    open_left, open_right = sides(numbers)
    collect(parts, total)
    for r in range(5):
        at = [moment_row(rows, k, r) for k in range(2)]
        moments[r : r + 1, :] = total[at[0] : at[0] + 1, :] + total[at[1] : at[1] + 1, :]
    ghosts = [jnp.sum(side[:, vels:].astype(F32), axis=1, keepdims=True) for side in (left, right)]
    r = diagonal(restitution[...], HALO, rows)
    state[0, 0:rows, :] = jnp.broadcast_to(r, (rows, LANES))
    state[0, 0:HALO, :] = jnp.broadcast_to(ghosts[0], (HALO, LANES))
    state[0, HALO + cells : rows, :] = jnp.broadcast_to(ghosts[1], (HALO, LANES))
    energy_row_in = energy_of(total, 0)
    base = sum(
        parts[0, at : at + 1, :].astype(F32) for at in (rows, moment_row(rows, 1, 0))
    )
    total[...] += moments[0:1, :]
    latent_layer(total, weights, b_latent, active)
    project(
        active[0:rows, :].astype(F32), moments, energy_row_in, state[0, :, 0:1],
        pats, consts, bands,
    )
    place = lax.broadcasted_iota(jnp.int32, (8, LANES), 0)
    cut_top = jnp.logical_and(place < HALO, jnp.logical_not(open_left))
    cut_bottom = jnp.logical_and(place >= 8 - HALO, jnp.logical_not(open_right))

    def decode_part(u, tile):
        span = slice(tile * LANES, (tile + group) * LANES)
        decoded[tile // group % SLOTS][...] = lax.dot_general(
            active[...], coders.at(u)[span, :], (((1,), (1,)), ((), ())),
            preferred_element_type=F32,
        )

    def encode(u):
        sums[...] += jnp.dot(
            cells_out.at(u)[...], coders.at(u)[...], preferred_element_type=F32
        )

    def transport(i, u):
        source = cells_in.at(u)
        target = cells_out.at(u)
        for k in range(nb):
            block = numbers[offset + i * nb + k]
            along, sign, weights = taps(block)
            parity = lax.rem(block, 2)
            level = consts[0] + along * consts[1] + (along * along) * consts[2]
            total = energy[...]
            for t in range(tiles):
                tile = k * tiles + t
                if tile % group == 0:
                    decode_part(u, tile)
                lanes = slice(tile * LANES, (tile + 1) * LANES)
                far = pl.ds(pl.multiple_of(i * width + tile * LANES, LANES), LANES)
                fill(pad, tile, lanes, far, source, left, right, inflow, open_left, open_right)
                fstar = stencil(pad, tile, 8 - HALO, rows, sign, weights)
                full = fstar + (
                    SCALE * decoded[tile // group % SLOTS][0:rows, slice(tile % group * LANES, (tile % group + 1) * LANES)]
                    - (level + bands[parity, t])
                )
                ghost = inflow[:, far]
                state[tile, 0:8, :] = jnp.where(cut_top, ghost, full[0:8])
                state[tile, 8 : rows - 8, :] = full[8 : rows - 8]
                state[tile, rows - 8 : rows, :] = jnp.where(cut_bottom, ghost, full[rows - 8 :])
                again = stencil(state, tile, HALO, cells, sign, weights)
                y, z = pattern_rows(pats, parity, slice(t * LANES, (t + 1) * LANES))
                total = total + again * (along * along + (y * y + z * z))
                target[:, lanes] = again.astype(BF16)
            energy[...] = total

    def step(i, u):
        cells_in.wait(i, u)
        coders.wait(i, u)
        coders.start(i + ahead, u + ahead)
        cells_in.start(i + ahead, u + ahead)
        cells_out.drain(i, u)
        transport(i, u)
        encode(u)
        cells_out.start(i, u)

    unrolled(steps, coders.slots, step)
    message[0:cells, :] = (sums[...] - base).astype(BF16)
    put_parts(message, lambda k, r: cells, energy_row(energy[...], cells), 3, LANES)
    for i in range(max(0, steps - cells_out.slots), steps):
        cells_out.wait(i, i)


def third_kernel(
    nb, offset, peers, numbers_in, source, coder, w_latent, b_latent, moments, restitution, *refs
):
    parts_in, refs = refs[:peers], refs[peers:]
    (
        out, result, pats, total, active, consts, bands,
        weights, parts, numbers, sem_s, tiles_c, sem_c, tiles_d, sem_d, sem_o, *decoded,
    ) = refs
    cells = source.shape[0]
    width = nb * WIDTH
    tiles = WIDTH // LANES
    wait = loads(
        [(part, parts.at[k]) for k, part in enumerate(parts_in)]
        + [(w_latent, weights), (numbers_in, numbers)],
        sem_s,
    )
    coders = Stream(coder, tiles_c, sem_c, width, 0)
    cells_in = Stream(source, tiles_d, sem_d, width, 1)
    cells_out = Stream(out, result, sem_o, width, 1, inward=False)
    ahead = coders.slots - 1
    coders.begin(ahead)
    cells_in.begin(ahead)
    steps = coders.count
    group = 3 if nb * tiles % 2 else 2

    moment_pattern(pats)
    wait()
    collect(parts, total)
    energy_row_in = energy_of(total, cells)
    total[...] += moments[0:1, :]
    latent_layer(total, weights, b_latent, active)
    project(
        active[0:cells, :].astype(F32), moments, energy_row_in,
        diagonal(restitution[...], 0, cells), pats, consts, bands,
    )

    def decode_part(u, tile):
        span = slice(tile * LANES, (tile + group) * LANES)
        decoded[tile // group % SLOTS][...] = lax.dot_general(
            active[0:cells, :], coders.at(u)[span, :], (((1,), (1,)), ((), ())),
            preferred_element_type=F32,
        )

    def finish(i, u):
        here = cells_in.at(u)
        target = cells_out.at(u)
        for k in range(nb):
            block = numbers[offset + i * nb + k]
            along = (2 * (block * WIDTH // (VGRID * VGRID)) + 1 - VGRID).astype(F32)
            parity = lax.rem(block, 2)
            level = consts[0] + along * consts[1] + (along * along) * consts[2]
            for t in range(tiles):
                tile = k * tiles + t
                if tile % group == 0:
                    decode_part(u, tile)
                lanes = slice(tile * LANES, (tile + 1) * LANES)
                full = here[:, lanes].astype(F32) + (
                    SCALE * decoded[tile // group % SLOTS][:, slice(tile % group * LANES, (tile % group + 1) * LANES)]
                    - (level + bands[parity, t])
                )
                target[:, lanes] = full.astype(BF16)

    def step(i, u):
        cells_in.wait(i, u)
        coders.wait(i, u)
        coders.start(i + ahead, u + ahead)
        cells_in.start(i + ahead, u + ahead)
        cells_out.drain(i, u)
        finish(i, u)
        cells_out.start(i, u)

    unrolled(steps, coders.slots, step)
    for i in range(max(0, steps - cells_out.slots), steps):
        cells_out.wait(i, i)


def shifted(array, axes, count, shift):
    return lax.ppermute(array, axes, [(i, (i + shift) % count) for i in range(count)])


def pieces(values):
    first = lax.reduce_precision(values, 8, 7)
    second = lax.reduce_precision(values - first, 8, 7)
    third = values - first - second
    return jnp.stack([first, second, third], -1).astype(BF16)


def spread(message):
    count = lax.axis_size("vel")
    return [message] + [shifted(message, "vel", count, s) for s in range(1, count)]


def body(density, coder, w_latent, b_latent, restitution, inflow, flags, blocks):
    cells, vels = density.shape
    count = blocks.shape[0]
    tiles = WIDTH // LANES
    rows = cells + 2 * HALO
    ring = ("cell", "sub")
    ring_count = lax.axis_size("cell") * lax.axis_size("sub")
    peers = lax.axis_size("vel")

    def edge(part, r):
        extra = jnp.pad(pieces(r), ((0, 0), (0, LANES - 3)))
        return jnp.concatenate([part, extra], 1)

    left = shifted(edge(density[cells - HALO :], restitution[cells - HALO :]), ring, ring_count, 1)
    right = shifted(edge(density[:HALO], restitution[:HALO]), ring, ring_count, -1)
    inflow = jnp.pad(inflow[None, :], ((0, 0), (0, LANES)))
    restitution = restitution[None, :]
    b_latent = b_latent[None, :]

    shape = jax.ShapeDtypeStruct
    vmem = pl.BlockSpec(memory_space=pltpu.VMEM)
    hbm = pl.BlockSpec(memory_space=pltpu.HBM)
    free = pl.BlockSpec(memory_space=pl.ANY)
    numbers = jnp.concatenate([flags, blocks])
    counts = pltpu.SMEM(numbers.shape, jnp.int32)
    offset = flags.shape[0]
    limit = VMEM_MIB * 1024 * 1024
    params = pltpu.CompilerParams(vmem_limit_bytes=limit)
    spaced = pltpu.CompilerParams(
        vmem_limit_bytes=limit
    )
    dma = pltpu.SemaphoreType.DMA

    def rings(nb, slots):
        width = nb * WIDTH
        return [
            pltpu.VMEM((slots, width, LATENT), BF16), dma((slots,)),
            pltpu.VMEM((slots, cells, width), BF16), dma((slots,)),
        ]

    def tiling(*choices):
        return next((nb, slots) for nb, slots in choices + ((1, 3),) if count % nb == 0)

    edges = [pltpu.VMEM((HALO, vels + LANES), BF16)] * 2 + [pltpu.VMEM((1, vels + LANES), F32)]
    latent_in = pltpu.VMEM((LATENT, LATENT), BF16)
    nb, slots = tiling((2, 4))
    width = nb * WIDTH

    message = pl.pallas_call(
        functools.partial(first_kernel, nb, offset),
        out_shape=shape((rows + 8, LATENT), BF16),
        in_specs=[free, hbm, free, free, free, hbm],
        out_specs=vmem,
        scratch_shapes=[
            pltpu.VMEM((nb * tiles, rows + 8, LANES), F32),
            pltpu.VMEM((rows + 8, width), BF16),
            pltpu.VMEM((rows + 8, width), BF16),
            pltpu.VMEM((rows, LANES), F32),
            pltpu.VMEM((8, WIDTH), F32),
            pltpu.VMEM((rows + 8, LATENT), F32),
            counts,
            *edges,
            dma((4,)),
            *rings(nb, slots),
        ],
        compiler_params=spaced,
        name="first",
    )(numbers, density, left, right, inflow, coder)

    nb, slots = tiling((4, 3), (2, 4))
    width = nb * WIDTH
    group = 3 if nb * tiles % 2 else 2
    coarse, message, moments = pl.pallas_call(
        functools.partial(second_kernel, nb, offset, peers),
        out_shape=(
            shape((cells, vels), BF16), shape((cells + 8, LATENT), BF16), shape((8, LATENT), F32),
        ),
        in_specs=[free, hbm, free, free, free, hbm, free, vmem, vmem] + [free] * peers,
        out_specs=(hbm, vmem, vmem),
        scratch_shapes=[
            pltpu.VMEM((nb * tiles, rows + 8, LANES), F32),
            pltpu.VMEM((nb * tiles, rows, LANES), F32),
            pltpu.VMEM((2, cells, width), BF16),
            pltpu.VMEM((cells, LANES), F32),
            pltpu.VMEM((8, WIDTH), F32),
            pltpu.VMEM((cells, LATENT), F32),
            pltpu.VMEM((rows + 8, LATENT), F32),
            pltpu.VMEM((rows + 8, LATENT), BF16),
            pltpu.VMEM((3, rows, LANES), F32),
            pltpu.VMEM((2, WIDTH // LANES, rows, LANES), F32),
            latent_in,
            pltpu.VMEM((peers, rows + 8, LATENT), BF16),
            counts,
            *edges,
            dma((peers + 5,)),
            *rings(nb, slots),
            dma((2,)),
            *[pltpu.VMEM((rows + 8, group * LANES), F32)] * SLOTS,
        ],
        compiler_params=params,
        name="second",
    )(
        numbers, density, left, right, inflow, coder, w_latent, b_latent, restitution,
        *spread(message),
    )

    nb, slots = tiling((2, 4))
    width = nb * WIDTH
    group = 3 if nb * tiles % 2 else 2
    return pl.pallas_call(
        functools.partial(third_kernel, nb, offset, peers),
        out_shape=shape((cells, vels), BF16),
        in_specs=[free, hbm, hbm, free, vmem, vmem, vmem] + [free] * peers,
        out_specs=hbm,
        scratch_shapes=[
            pltpu.VMEM((2, cells, width), BF16),
            pltpu.VMEM((8, WIDTH), F32),
            pltpu.VMEM((cells + 8, LATENT), F32),
            pltpu.VMEM((cells + 8, LATENT), BF16),
            pltpu.VMEM((3, cells, LANES), F32),
            pltpu.VMEM((2, WIDTH // LANES, cells, LANES), F32),
            latent_in,
            pltpu.VMEM((peers, cells + 8, LATENT), BF16),
            counts,
            dma((peers + 2,)),
            *rings(nb, slots),
            dma((2,)),
            *[pltpu.VMEM((cells, group * LANES), F32)] * SLOTS,
        ],
        compiler_params=params,
        name="third",
    )(numbers, coarse, coder, w_latent, b_latent, moments, restitution, *spread(message))


def solution(mesh):
    return jax.shard_map(
        body,
        mesh=mesh,
        in_specs=(
            P(("groups", "cell", "sub"), "vel"),
            P("vel", None),
            P(),
            P(),
            P(("groups", "cell", "sub")),
            P(("groups", "vel")),
            P("groups"),
            P(("groups", "vel")),
        ),
        out_specs=P(("groups", "cell", "sub"), "vel"),
        check_vma=False,
    )
```

```python
import functools
import math

import jax
import jax.numpy as jnp
import numpy as np
from jax import lax
from jax.experimental import pallas as pl
from jax.experimental.pallas import tpu as pltpu
from jax.sharding import PartitionSpec as P

VGRID = 48
LATENT = 512
VBLOCKS = 96
STEPS = 2
VELS = 110592
WIDTH = VELS // VBLOCKS
LANES = 128
HALO = 4
SLOTS = 3
VMEM_MIB = 50
FIRST_MIB = 50
SINK_RATE = 0.5
COURANT = 0.9
SCALE = math.sqrt(VELS / LATENT)
F32 = jnp.float32
BF16 = jnp.bfloat16


def grid_moments():
    centres = (2.0 * np.arange(VGRID) + 1.0 - VGRID) / VGRID
    second = float(np.sum(centres**2))
    fourth = float(np.sum(centres**4))
    number = float(VGRID)
    total = number**3
    cross = 3.0 * number * number * second
    quartic = 3.0 * number * number * fourth + 6.0 * number * second * second
    square = number * number * second
    return (total, cross, quartic, square)


def moment_pattern(pats):
    number = lax.broadcasted_iota(jnp.int32, (1, WIDTH), 1).astype(F32)
    along_y = jnp.floor((number + 0.5) * (1.0 / VGRID))
    along_z = number - VGRID * along_y
    first = 2.0 * along_y + (1 - VGRID)
    pats[0:1, :] = first
    pats[1:2, :] = first + (2 * WIDTH // VGRID)
    pats[2:3, :] = 2.0 * along_z + (1 - VGRID)


def taps(block):
    along = 2 * (block * WIDTH // (VGRID * VGRID)) + 1 - VGRID
    sign = jnp.where(along >= 0, 1, -1)
    along = along.astype(F32)
    a = jnp.abs(along) * (COURANT / VGRID)
    upwind = (1.0 - a) * 0.5
    curved = (1.0 - a * a) * (1.0 / 6.0)
    far = -a * curved
    behind = a * (1.0 - upwind + 3.0 * curved)
    here = 1.0 - a * (1.0 - 2.0 * upwind + 3.0 * curved)
    ahead = -a * (upwind - curved)
    return along, sign, (far, behind, here, ahead)


def stencil(ref, tile, first, count, sign, weights):
    far, behind, here, ahead = weights
    at = lambda shift: ref[tile, pl.ds(first + shift, count), :]
    return (
        far * at(-2 * sign) + behind * at(-sign) + here * at(0) + ahead * at(sign)
    )


def fill(pad, tile, lanes, far_lanes, density, left, right, inflow, open_left, open_right):
    cells = density.shape[0]
    ghost = inflow[:, far_lanes]
    pad[tile, 8 : 8 + cells, :] = density[:, lanes].astype(F32)
    pad[tile, 8 - HALO : 8, :] = jnp.where(open_left, left[:, far_lanes].astype(F32), ghost)
    pad[tile, 8 + cells : 8 + cells + HALO, :] = jnp.where(
        open_right, right[:, far_lanes].astype(F32), ghost
    )


def energy_row(total, rows):
    column = jnp.sum(total, axis=1, keepdims=True) * (1.0 / (VGRID * VGRID))
    row = lax.broadcasted_iota(jnp.int32, (rows, LANES), 0)
    lane = lax.broadcasted_iota(jnp.int32, (rows, LANES), 1)
    return jnp.sum(jnp.where(row == lane, column, 0.0), axis=0, keepdims=True)


def pattern_rows(pats, parity, lanes):
    y = jnp.where(parity == 0, pats[0:1, lanes], pats[1:2, lanes])
    return y, pats[2:3, lanes]


def sides(flags):
    sub_count = lax.axis_size("sub")
    count = lax.axis_size("cell") * sub_count
    position = lax.axis_index("cell") * sub_count + lax.axis_index("sub")
    return flags[position] == 1, flags[lax.rem(position + 1, count)] == 1


class Stream:
    def __init__(self, source, buffers, sems, tile, axis, inward=True):
        self.source, self.buffers, self.sems = source, buffers, sems
        self.tile, self.axis, self.inward = tile, axis, inward
        self.count = source.shape[axis] // tile
        self.slots = buffers.shape[0]

    def copy(self, i, u):
        slot = u % self.slots
        span = pl.ds(pl.multiple_of(i * self.tile, LANES), self.tile)
        far = self.source.at[span, :] if self.axis == 0 else self.source.at[:, span]
        near = self.buffers.at[slot]
        source, target = (far, near) if self.inward else (near, far)
        return pltpu.make_async_copy(source, target, self.sems.at[slot])

    def begin(self, ahead):
        for i in range(min(ahead, self.count)):
            self.copy(i, i).start()

    def start(self, i, u):
        if isinstance(i, int):
            if i < self.count:
                self.copy(i, u).start()
        else:

            @pl.when(i < self.count)
            def _():
                self.copy(i, u).start()

    def wait(self, i, u):
        self.copy(i, u).wait()

    def drain(self, i, u):
        if isinstance(i, int):
            if i >= self.slots:
                self.wait(i - self.slots, u)
        else:

            @pl.when(i >= self.slots)
            def _():
                self.wait(i - self.slots, u)

    def at(self, u):
        return self.buffers.at[u % self.slots]


def unrolled(last, ring, step):
    first, trips = 0, last // ring
    if trips > 1:

        def trip(j, carry):
            for k in range(ring):
                step(ring * j + k, k)
            return carry

        lax.fori_loop(0, trips, trip, 0)
        first = ring * trips
    for i in range(first, last):
        step(i, i % ring)


def loads(pairs, sems):
    copies = [pltpu.make_async_copy(a, b, sems.at[k]) for k, (a, b) in enumerate(pairs)]
    for copy in copies:
        copy.start()

    def wait():
        for copy in copies:
            copy.wait()

    return wait


def put_parts(message, row_of, values, count, lane_step=0):
    height, width = values.shape
    for k in range(count):
        part = values.astype(BF16)
        values = values - part.astype(F32)
        for r in range(height):
            lanes = slice(k * lane_step, k * lane_step + width)
            message[row_of(k, r) : row_of(k, r) + 1, lanes] = part[r : r + 1]


def moment_row(rows, k, r):
    place = 5 * k + r
    return rows + place if place < 8 else rows - 2 + (place - 8)


def first_kernel(
    nb, offset, numbers_in, density, left_in, right_in, inflow_in, coder, message, *refs
):
    (
        pad, coarse_a, coarse_b, energy, pats, sums, numbers, left, right, inflow, sem_s,
        tiles_c, sem_c, tiles_d, sem_d,
    ) = refs
    cells = density.shape[0]
    rows = cells + 2 * HALO
    width = nb * WIDTH
    tiles = WIDTH // LANES
    coders = Stream(coder, tiles_c, sem_c, width, 0)
    cells_in = Stream(density, tiles_d, sem_d, width, 1)
    cells_in.begin(1)
    wait = loads(
        (
            (left_in, left), (right_in, right), (inflow_in, inflow),
            (numbers_in, numbers),
        ),
        sem_s,
    )
    ahead = coders.slots - 1
    coders.begin(ahead)
    for i in range(1, min(ahead, cells_in.count)):
        cells_in.copy(i, i).start()
    steps = coders.count
    coarse = (coarse_a, coarse_b)

    moment_pattern(pats)
    sums[...] = jnp.zeros_like(sums)
    energy[...] = jnp.zeros_like(energy)
    pad[...] = jnp.zeros_like(pad)
    wait()
    open_left, open_right = sides(numbers)
    kind = lax.broadcasted_iota(jnp.int32, (8, LANES), 0)

    def transport(i, u):
        source = cells_in.at(u)
        for k in range(nb):
            block = numbers[offset + i * nb + k]
            along, sign, weights = taps(block)
            parity = lax.rem(block, 2)
            total = energy[...]
            for t in range(tiles):
                tile = k * tiles + t
                lanes = slice(tile * LANES, (tile + 1) * LANES)
                far = pl.ds(pl.multiple_of(i * width + tile * LANES, LANES), LANES)
                fill(pad, tile, lanes, far, source, left, right, inflow, open_left, open_right)
                fstar = stencil(pad, tile, 8 - HALO, rows, sign, weights)
                y, z = pattern_rows(pats, parity, slice(t * LANES, (t + 1) * LANES))
                e = along * along + (y * y + z * z)
                total = total + fstar * e
                high = e.astype(BF16).astype(F32)
                basis = jnp.where(kind == 0, 1.0, 0.0)
                basis = jnp.where(kind == 1, along, basis)
                basis = jnp.where(kind == 2, y, basis)
                basis = jnp.where(kind == 3, z, basis)
                basis = jnp.where(kind == 4, high, basis)
                basis = jnp.where(kind == 5, e - high, basis)
                coarse[u % 2][:, lanes] = jnp.concatenate([fstar, basis], 0).astype(BF16)
            energy[...] = total

    def encode(u):
        sums[...] += jnp.dot(coarse[u % 2][...], coders.at(u)[...], preferred_element_type=F32)

    def step(i, u):
        cells_in.wait(i, u)
        coders.wait(i, u)
        coders.start(i + ahead, u + ahead)
        cells_in.start(i + ahead, u + ahead)
        transport(i, u)
        encode(u)

    unrolled(steps, coders.slots, step)

    base = sums[rows : rows + 1, :]
    base = base.astype(BF16).astype(F32) + (base - base.astype(BF16).astype(F32)).astype(BF16)
    message[0:rows, :] = (sums[0:rows, :] - base).astype(BF16)
    last = sums[rows + 4 : rows + 5, :] + sums[rows + 5 : rows + 6, :]
    moments = jnp.concatenate([sums[rows : rows + 4, :], last], 0)
    put_parts(message, functools.partial(moment_row, rows), moments, 2)
    put_parts(message, lambda k, r: 0, energy_row(energy[...], rows), 3, LANES)


def project(act, moments, energy, restitution, pats, consts, bands):
    total, cross, quartic, square = grid_moments()
    determinant = total * quartic - cross * cross
    rows = restitution.shape[0]
    inverse = 1.0 / VGRID
    dots = [
        SCALE * jnp.sum(act * moments[k : k + 1, :], axis=1, keepdims=True) for k in range(5)
    ]
    row = lax.broadcasted_iota(jnp.int32, (rows, LANES), 0)
    lane = lax.broadcasted_iota(jnp.int32, (rows, LANES), 1)
    energy_sum = jnp.sum(jnp.where(row == lane, energy, 0.0), axis=1, keepdims=True)
    sink = -SINK_RATE * (1.0 - restitution * restitution) * energy_sum
    excess = dots[4] * (inverse * inverse) - sink
    mass = (quartic * dots[0] - cross * excess) / determinant
    power = (total * excess - cross * dots[0]) / determinant * (inverse * inverse)
    slopes = [dots[k] * (inverse * inverse / square) for k in (1, 2, 3)]
    spread = lambda column: jnp.broadcast_to(column, (rows, LANES))
    consts[0] = spread(mass)
    consts[1] = spread(slopes[0])
    consts[2] = spread(power)
    power, second, third = spread(power), spread(slopes[1]), spread(slopes[2])
    for parity in range(2):
        for t in range(WIDTH // LANES):
            lanes = slice(t * LANES, (t + 1) * LANES)
            y, z = pats[parity : parity + 1, lanes], pats[2:3, lanes]
            bands[parity, t] = second * y + third * z + power * (y * y + z * z)


def diagonal(row, first, rows):
    shape = (rows, row.shape[1])
    place = lax.broadcasted_iota(jnp.int32, shape, 0) - first
    lane = lax.broadcasted_iota(jnp.int32, shape, 1)
    return jnp.sum(jnp.where(place == lane, row, 0.0), axis=1, keepdims=True)


def collect(parts, total):
    total[...] = sum(parts[k].astype(F32) for k in range(parts.shape[0]))


def energy_of(total, row):
    return sum(total[row : row + 1, k * LANES : (k + 1) * LANES] for k in range(3))


def latent_layer(total, w_latent, b_latent, active):
    mixed = jnp.dot(total[...].astype(BF16), w_latent[...], preferred_element_type=F32)
    active[...] = jnp.tanh(mixed + b_latent[...]).astype(BF16)


def diagonal(row, first, rows):
    shape = (rows, row.shape[1])
    place = lax.broadcasted_iota(jnp.int32, shape, 0) - first
    lane = lax.broadcasted_iota(jnp.int32, shape, 1)
    return jnp.sum(jnp.where(place == lane, row, 0.0), axis=1, keepdims=True)


def second_kernel(
    nb, offset, peers, numbers_in, density, left_in, right_in, inflow_in, coder, w_latent,
    b_latent, restitution, *refs
):
    parts_in, refs = refs[:peers], refs[peers:]
    (
        out, message, moments, pad, state, coarse, energy, pats, sums,
        total, active, consts, bands, weights, parts, numbers, left, right, inflow, sem_s,
        tiles_c, sem_c, tiles_d, sem_d, sem_o, *decoded,
    ) = refs
    cells = density.shape[0]
    rows = cells + 2 * HALO
    width = nb * WIDTH
    tiles = WIDTH // LANES
    wait = loads(
        [(part, parts.at[k]) for k, part in enumerate(parts_in)]
        + [(w_latent, weights), (left_in, left), (right_in, right), (inflow_in, inflow)]
        + [(numbers_in, numbers)],
        sem_s,
    )
    coders = Stream(coder, tiles_c, sem_c, width, 0)
    cells_in = Stream(density, tiles_d, sem_d, width, 1)
    cells_out = Stream(out, coarse, sem_o, width, 1, inward=False)
    ahead = coders.slots - 1
    coders.begin(ahead)
    cells_in.begin(ahead)
    steps = coders.count
    group = 3 if nb * tiles % 2 else 2
    vels = density.shape[1]

    moment_pattern(pats)
    sums[...] = jnp.zeros_like(sums)
    energy[...] = jnp.zeros_like(energy)
    pad[...] = jnp.zeros_like(pad)
    wait()
    open_left, open_right = sides(numbers)
    collect(parts, total)
    for r in range(5):
        at = [moment_row(rows, k, r) for k in range(2)]
        moments[r : r + 1, :] = total[at[0] : at[0] + 1, :] + total[at[1] : at[1] + 1, :]
    ghosts = [jnp.sum(side[:, vels:].astype(F32), axis=1, keepdims=True) for side in (left, right)]
    r = diagonal(restitution[...], HALO, rows)
    state[0, 0:rows, :] = jnp.broadcast_to(r, (rows, LANES))
    state[0, 0:HALO, :] = jnp.broadcast_to(ghosts[0], (HALO, LANES))
    state[0, HALO + cells : rows, :] = jnp.broadcast_to(ghosts[1], (HALO, LANES))
    energy_row_in = energy_of(total, 0)
    base = sum(
        parts[0, at : at + 1, :].astype(F32) for at in (rows, moment_row(rows, 1, 0))
    )
    total[...] += moments[0:1, :]
    latent_layer(total, weights, b_latent, active)
    project(
        active[0:rows, :].astype(F32), moments, energy_row_in, state[0, :, 0:1],
        pats, consts, bands,
    )
    place = lax.broadcasted_iota(jnp.int32, (8, LANES), 0)
    cut_top = jnp.logical_and(place < HALO, jnp.logical_not(open_left))
    cut_bottom = jnp.logical_and(place >= 8 - HALO, jnp.logical_not(open_right))

    def decode_part(u, tile):
        span = slice(tile * LANES, (tile + group) * LANES)
        decoded[tile // group % SLOTS][...] = lax.dot_general(
            active[...], coders.at(u)[span, :], (((1,), (1,)), ((), ())),
            preferred_element_type=F32,
        )

    def encode(u):
        sums[...] += jnp.dot(
            cells_out.at(u)[...], coders.at(u)[...], preferred_element_type=F32
        )

    def transport(i, u):
        source = cells_in.at(u)
        target = cells_out.at(u)
        for k in range(nb):
            block = numbers[offset + i * nb + k]
            along, sign, weights = taps(block)
            parity = lax.rem(block, 2)
            level = consts[0] + along * consts[1] + (along * along) * consts[2]
            total = energy[...]
            for t in range(tiles):
                tile = k * tiles + t
                if tile % group == 0:
                    decode_part(u, tile)
                lanes = slice(tile * LANES, (tile + 1) * LANES)
                far = pl.ds(pl.multiple_of(i * width + tile * LANES, LANES), LANES)
                fill(pad, tile, lanes, far, source, left, right, inflow, open_left, open_right)
                fstar = stencil(pad, tile, 8 - HALO, rows, sign, weights)
                full = fstar + (
                    SCALE * decoded[tile // group % SLOTS][0:rows, slice(tile % group * LANES, (tile % group + 1) * LANES)]
                    - (level + bands[parity, t])
                )
                ghost = inflow[:, far]
                state[tile, 0:8, :] = jnp.where(cut_top, ghost, full[0:8])
                state[tile, 8 : rows - 8, :] = full[8 : rows - 8]
                state[tile, rows - 8 : rows, :] = jnp.where(cut_bottom, ghost, full[rows - 8 :])
                again = stencil(state, tile, HALO, cells, sign, weights)
                y, z = pattern_rows(pats, parity, slice(t * LANES, (t + 1) * LANES))
                total = total + again * (along * along + (y * y + z * z))
                target[:, lanes] = again.astype(BF16)
            energy[...] = total

    def step(i, u):
        cells_in.wait(i, u)
        coders.wait(i, u)
        coders.start(i + ahead, u + ahead)
        cells_in.start(i + ahead, u + ahead)
        cells_out.drain(i, u)
        transport(i, u)
        encode(u)
        cells_out.start(i, u)

    unrolled(steps, coders.slots, step)
    message[0:cells, :] = (sums[...] - base).astype(BF16)
    put_parts(message, lambda k, r: cells, energy_row(energy[...], cells), 3, LANES)
    for i in range(max(0, steps - cells_out.slots), steps):
        cells_out.wait(i, i)


def third_kernel(
    nb, offset, peers, numbers_in, source, coder, w_latent, b_latent, moments, restitution, *refs
):
    parts_in, refs = refs[:peers], refs[peers:]
    (
        out, result, pats, total, active, consts, bands,
        weights, parts, numbers, sem_s, tiles_c, sem_c, tiles_d, sem_d, sem_o, *decoded,
    ) = refs
    cells = source.shape[0]
    width = nb * WIDTH
    tiles = WIDTH // LANES
    wait = loads(
        [(part, parts.at[k]) for k, part in enumerate(parts_in)]
        + [(w_latent, weights), (numbers_in, numbers)],
        sem_s,
    )
    coders = Stream(coder, tiles_c, sem_c, width, 0)
    cells_in = Stream(source, tiles_d, sem_d, width, 1)
    cells_out = Stream(out, result, sem_o, width, 1, inward=False)
    ahead = coders.slots - 1
    coders.begin(ahead)
    cells_in.begin(ahead)
    steps = coders.count
    group = 3 if nb * tiles % 2 else 2

    moment_pattern(pats)
    wait()
    collect(parts, total)
    energy_row_in = energy_of(total, cells)
    total[...] += moments[0:1, :]
    latent_layer(total, weights, b_latent, active)
    project(
        active[0:cells, :].astype(F32), moments, energy_row_in,
        diagonal(restitution[...], 0, cells), pats, consts, bands,
    )

    def decode_part(u, tile):
        span = slice(tile * LANES, (tile + group) * LANES)
        decoded[tile // group % SLOTS][...] = lax.dot_general(
            active[0:cells, :], coders.at(u)[span, :], (((1,), (1,)), ((), ())),
            preferred_element_type=F32,
        )

    def finish(i, u):
        here = cells_in.at(u)
        target = cells_out.at(u)
        for k in range(nb):
            block = numbers[offset + i * nb + k]
            along = (2 * (block * WIDTH // (VGRID * VGRID)) + 1 - VGRID).astype(F32)
            parity = lax.rem(block, 2)
            level = consts[0] + along * consts[1] + (along * along) * consts[2]
            for t in range(tiles):
                tile = k * tiles + t
                if tile % group == 0:
                    decode_part(u, tile)
                lanes = slice(tile * LANES, (tile + 1) * LANES)
                full = here[:, lanes].astype(F32) + (
                    SCALE * decoded[tile // group % SLOTS][:, slice(tile % group * LANES, (tile % group + 1) * LANES)]
                    - (level + bands[parity, t])
                )
                target[:, lanes] = full.astype(BF16)

    def step(i, u):
        cells_in.wait(i, u)
        coders.wait(i, u)
        coders.start(i + ahead, u + ahead)
        cells_in.start(i + ahead, u + ahead)
        cells_out.drain(i, u)
        finish(i, u)
        cells_out.start(i, u)

    unrolled(steps, coders.slots, step)
    for i in range(max(0, steps - cells_out.slots), steps):
        cells_out.wait(i, i)


def shifted(array, axes, count, shift):
    return lax.ppermute(array, axes, [(i, (i + shift) % count) for i in range(count)])


def pieces(values):
    values = jnp.broadcast_to(values[:, None], (values.shape[0], LANES))
    lane = lax.broadcasted_iota(jnp.int32, values.shape, 1)
    first = lax.reduce_precision(values, 8, 7)
    second = lax.reduce_precision(values - first, 8, 7)
    third = values - first - second
    parts = jnp.where(lane == 0, first, jnp.where(lane == 1, second, third))
    return jnp.where(lane < 3, parts, 0.0).astype(BF16)


def spread(message):
    count = lax.axis_size("vel")
    return [message] + [shifted(message, "vel", count, s) for s in range(1, count)]


def body(density, coder, w_latent, b_latent, restitution, inflow, flags, blocks):
    cells, vels = density.shape
    count = blocks.shape[0]
    tiles = WIDTH // LANES
    rows = cells + 2 * HALO
    ring = ("cell", "sub")
    ring_count = lax.axis_size("cell") * lax.axis_size("sub")
    peers = lax.axis_size("vel")

    def edge(part, r):
        return jnp.concatenate([part, pieces(r)], 1)

    left = shifted(edge(density[cells - HALO :], restitution[cells - HALO :]), ring, ring_count, 1)
    right = shifted(edge(density[:HALO], restitution[:HALO]), ring, ring_count, -1)
    inflow = jnp.pad(inflow[None, :], ((0, 0), (0, LANES)))
    restitution = restitution[None, :]
    b_latent = b_latent[None, :]

    shape = jax.ShapeDtypeStruct
    vmem = pl.BlockSpec(memory_space=pltpu.VMEM)
    hbm = pl.BlockSpec(memory_space=pltpu.HBM)
    free = pl.BlockSpec(memory_space=pl.ANY)
    numbers = jnp.concatenate([flags, blocks])
    counts = pltpu.SMEM(numbers.shape, jnp.int32)
    offset = flags.shape[0]
    limit = VMEM_MIB * 1024 * 1024
    params = pltpu.CompilerParams(vmem_limit_bytes=limit)
    spaced = pltpu.CompilerParams(
        vmem_limit_bytes=FIRST_MIB * 1024 * 1024
    )
    dma = pltpu.SemaphoreType.DMA

    def rings(nb, slots):
        width = nb * WIDTH
        return [
            pltpu.VMEM((slots, width, LATENT), BF16), dma((slots,)),
            pltpu.VMEM((slots, cells, width), BF16), dma((slots,)),
        ]

    def tiling(*choices):
        return next((nb, slots) for nb, slots in choices + ((1, 3),) if count % nb == 0)

    edges = [pltpu.VMEM((HALO, vels + LANES), BF16)] * 2 + [pltpu.VMEM((1, vels + LANES), F32)]
    latent_in = pltpu.VMEM((LATENT, LATENT), BF16)
    nb, slots = tiling((2, 4))
    width = nb * WIDTH

    message = pl.pallas_call(
        functools.partial(first_kernel, nb, offset),
        out_shape=shape((rows + 8, LATENT), BF16),
        in_specs=[free, hbm, free, free, free, hbm],
        out_specs=vmem,
        scratch_shapes=[
            pltpu.VMEM((nb * tiles, rows + 8, LANES), F32),
            pltpu.VMEM((rows + 8, width), BF16),
            pltpu.VMEM((rows + 8, width), BF16),
            pltpu.VMEM((rows, LANES), F32),
            pltpu.VMEM((8, WIDTH), F32),
            pltpu.VMEM((rows + 8, LATENT), F32),
            counts,
            *edges,
            dma((4,)),
            *rings(nb, slots),
        ],
        compiler_params=spaced,
        name="first",
    )(numbers, density, left, right, inflow, coder)

    nb, slots = tiling((4, 3), (2, 4))
    width = nb * WIDTH
    group = 3 if nb * tiles % 2 else 2
    coarse, message, moments = pl.pallas_call(
        functools.partial(second_kernel, nb, offset, peers),
        out_shape=(
            shape((cells, vels), BF16), shape((cells + 8, LATENT), BF16), shape((8, LATENT), F32),
        ),
        in_specs=[free, hbm, free, free, free, hbm, free, vmem, vmem] + [free] * peers,
        out_specs=(hbm, vmem, vmem),
        scratch_shapes=[
            pltpu.VMEM((nb * tiles, rows + 8, LANES), F32),
            pltpu.VMEM((nb * tiles, rows, LANES), F32),
            pltpu.VMEM((2, cells, width), BF16),
            pltpu.VMEM((cells, LANES), F32),
            pltpu.VMEM((8, WIDTH), F32),
            pltpu.VMEM((cells, LATENT), F32),
            pltpu.VMEM((rows + 8, LATENT), F32),
            pltpu.VMEM((rows + 8, LATENT), BF16),
            pltpu.VMEM((3, rows, LANES), F32),
            pltpu.VMEM((2, WIDTH // LANES, rows, LANES), F32),
            latent_in,
            pltpu.VMEM((peers, rows + 8, LATENT), BF16),
            counts,
            *edges,
            dma((peers + 5,)),
            *rings(nb, slots),
            dma((2,)),
            *[pltpu.VMEM((rows + 8, group * LANES), F32)] * SLOTS,
        ],
        compiler_params=params,
        name="second",
    )(
        numbers, density, left, right, inflow, coder, w_latent, b_latent, restitution,
        *spread(message),
    )

    nb, slots = tiling((2, 4))
    width = nb * WIDTH
    group = 3 if nb * tiles % 2 else 2
    return pl.pallas_call(
        functools.partial(third_kernel, nb, offset, peers),
        out_shape=shape((cells, vels), BF16),
        in_specs=[free, hbm, hbm, free, vmem, vmem, vmem] + [free] * peers,
        out_specs=hbm,
        scratch_shapes=[
            pltpu.VMEM((2, cells, width), BF16),
            pltpu.VMEM((8, WIDTH), F32),
            pltpu.VMEM((cells + 8, LATENT), F32),
            pltpu.VMEM((cells + 8, LATENT), BF16),
            pltpu.VMEM((3, cells, LANES), F32),
            pltpu.VMEM((2, WIDTH // LANES, cells, LANES), F32),
            latent_in,
            pltpu.VMEM((peers, cells + 8, LATENT), BF16),
            counts,
            dma((peers + 2,)),
            *rings(nb, slots),
            dma((2,)),
            *[pltpu.VMEM((cells, group * LANES), F32)] * SLOTS,
        ],
        compiler_params=params,
        name="third",
    )(numbers, coarse, coder, w_latent, b_latent, moments, restitution, *spread(message))


def solution(mesh):
    return jax.shard_map(
        body,
        mesh=mesh,
        in_specs=(
            P(("groups", "cell", "sub"), "vel"),
            P("vel", None),
            P(),
            P(),
            P(("groups", "cell", "sub")),
            P(("groups", "vel")),
            P("groups"),
            P(("groups", "vel")),
        ),
        out_specs=P(("groups", "cell", "sub"), "vel"),
        check_vma=False,
    )
```
